32 devices in a mesh: shard: 8 (over y, x, core), rep: 4 (over z).
Axes of the slice: x: 2, y: 2, z: 4, core: 2. Of those that a mesh axis runs over, the one named last changes fastest.
Arguments:
- pooled_grad: float32 [128, 4, 8, 256], P('shard', 'rep'), may hold values from -0.8 to 0.8
- bag_lengths: int32 [8, 4, 128], P('shard', 'rep'), may hold values from 1 to 64, 2048 in all within a row
- row_slots: int32 [8, 4, 2048], P('shard', 'rep'), may hold values from 0 to 511
- id_weights: int32 [8, 4, 2048], P('shard', 'rep'), may hold values from 1 to 32
- touched_rows: float32 [8, 512, 256], P('shard'), may hold values from -6 to 6
- accumulator: float32 [8, 512], P('shard'), may hold values from 0.005 to 0.5
Outputs:
- row_grad: float32 [8, 512, 256], P('shard', 'rep')
- updated_rows: float32 [8, 512, 256], P('shard')
The draws below stay inside these ranges and needn't reach their ends.
Inputs may be any that keep to these rules, and one draw needn't show every extreme that they name: `bag_lengths`: in each table and replica group the bag lengths sum to 2048.
All inputs are finite; a program needn't handle non-finite values.
Results may differ from the reference program's by a relative error of at most 0.0003.
Values sent between devices are 32-bit elements; how exact they have to be, the bound alone decides.
A program may use at most 64 MiB of HBM per device.

```python
import math
import jax
import jax.numpy as jnp
import numpy as np
from jax import lax

E = 256
MOST = 64
SLOTS = 512
TABLES = 8
REPS = 4
SH_SAMPLES = 128
ENTRIES = 2048


def with_ends(result, own_key, low, top_value):
    longest = result.shape.index(max(result.shape))
    spots = []
    for shift in (0, 1):
        where = [jax.random.randint(jax.random.fold_in(own_key, axis), (), 0, length) for axis, length in enumerate(result.shape)]
        where[longest] = (where[longest] + shift) % result.shape[longest]
        spots.append(tuple(where))
    return result.at[spots[0]].set(low).at[spots[1]].set(top_value)


def level_of(rng, extent, cuts, smallest, top_value):
    factor_of, own = 1.0, jax.random.fold_in(rng, 6)
    for dim, parts in cuts:
        heights = jnp.exp(jax.random.uniform(jax.random.fold_in(own, dim), (parts,), jnp.float32, smallest / len(cuts), top_value / len(cuts)))
        factor_of = factor_of * jnp.repeat(heights, extent[dim] // parts).reshape([-1 if axis == dim else 1 for axis in range(len(extent))])
    return factor_of


def rank_table(count, slope):
    portions = [(1 << 20) // math.isqrt(rank ** slope) + 1 for rank in range(1, count + 1)]
    scale = 1 + sum(portions) // (1 << 30)
    return np.cumsum(np.array([max(1, weight // scale) for weight in portions]))


def ranked(stream_key, dims, amount, lean):
    table = rank_table(amount, lean)
    pick = jax.random.randint(jax.random.fold_in(stream_key, 1), dims, 0, int(table[amount - 1]))
    grade = jnp.searchsorted(jnp.asarray(table, jnp.int32), pick, side="right")
    return jax.random.permutation(jax.random.fold_in(stream_key, 2), amount)[grade].astype(jnp.int32)


def length_profile(count, total, reach, skew):
    loads = [(1 << 20) // math.isqrt(standing ** skew) + 1 for standing in range(2, count + 1)]
    surplus, holding = total - reach - (count - 1), [1] * (count - 1)
    while surplus > 0:
        movable = [i for i in range(count - 1) if holding[i] < reach]
        mass, remaining = sum([loads[i] for i in movable]), surplus
        for i in movable:
            more = min(reach - holding[i], max(1, remaining * loads[i] // mass), surplus)
            holding[i] = holding[i] + more
            surplus = surplus - more
    return np.array([reach] + holding)


def uneven_parts(rng, number_of, total, bound, slope):
    if number_of == 2:
        one = jax.random.randint(rng, (), max(1, total - bound), min(bound, total - 1) + 1)
        return jnp.stack([one, total - one])
    sizes = jnp.asarray(length_profile(number_of, total, bound, slope), jnp.int32)
    pairs = (number_of - 1) // 2
    giver, sink = sizes[1:1 + 2 * pairs:2], sizes[2:2 + 2 * pairs:2]
    slack = jnp.minimum(giver - 1, bound - sink)
    moved = jax.random.randint(jax.random.fold_in(rng, 1), (pairs,), 0, 1 << 20) % (slack + 1)
    sizes = sizes.at[1:1 + 2 * pairs:2].set(giver - moved).at[2:2 + 2 * pairs:2].set(sink + moved)
    return sizes[jax.random.permutation(jax.random.fold_in(rng, 2), number_of)]


def scatter_about(key, extent, spread, limit, cuts=(), kind=jnp.bfloat16):
    result = spread * jax.random.normal(key, extent, jnp.float32)
    if cuts:
        result = result * level_of(key, extent, cuts, -0.22, 0.18)
    return jnp.clip(result, -limit, limit).astype(kind)


def setup_inputs(seed: int = 0) -> dict:
    key_of = jax.random.split(jax.random.key(seed), 7)
    pooled_grad = scatter_about(key_of[0], (SH_SAMPLES, REPS, TABLES, E), 0.1, 0.8, ((0, 8), (1, 4)), jnp.float32)
    bag_lengths = jax.vmap(lambda own: uneven_parts(own, SH_SAMPLES, ENTRIES, MOST, 2))(jax.random.split(key_of[1], TABLES * REPS)).reshape((TABLES, REPS, SH_SAMPLES)).astype(jnp.int32)
    row_slots = with_ends(ranked(key_of[2], (TABLES, REPS, ENTRIES), SLOTS, 2), jax.random.fold_in(key_of[2], 3), 0, SLOTS - 1).astype(jnp.int32)
    id_weights = with_ends(jax.random.randint(key_of[3], (TABLES, REPS, ENTRIES), 1, 33), jax.random.fold_in(key_of[3], 1), 1, 32).astype(jnp.int32)
    touched_rows = scatter_about(key_of[4], (TABLES, SLOTS, E), 1.0, 6.0, ((0, 8),), jnp.float32)
    accumulator = jnp.clip(jnp.exp(math.log(0.5) - 4.6051702 * jax.random.uniform(key_of[5], (TABLES, SLOTS), jnp.float32) ** level_of(key_of[5], (TABLES, SLOTS), ((0, 8),), -0.2, 0.2)), 0.005, 0.5)
    return {"pooled_grad": pooled_grad, "bag_lengths": bag_lengths, "row_slots": row_slots, "id_weights": id_weights, "touched_rows": touched_rows, "accumulator": accumulator}


learn_rate = 0.5

def one_table(index, pooled_grad, bag_lengths, row_slots, id_weights):
    total = jnp.zeros((SLOTS, E), jnp.float32)
    positions = jnp.arange(ENTRIES, dtype=jnp.int32)
    for group in range(REPS):
        ends = jnp.cumsum(bag_lengths[index, group]).astype(jnp.int32)
        bags = jnp.searchsorted(ends, positions, side='right').astype(jnp.int32)
        column = pooled_grad[:, group, index]
        scaled = id_weights[index, group].astype(jnp.float32) * 0.0625
        picked = jnp.take(column, bags, axis=0) * scaled[:, None]
        total = total + jax.ops.segment_sum(picked, row_slots[index, group], num_segments=SLOTS)
    return total

def reference(pooled_grad, bag_lengths, row_slots, id_weights, touched_rows, accumulator):
    grads = lax.map(lambda index: one_table(index, pooled_grad, bag_lengths, row_slots, id_weights), jnp.arange(TABLES, dtype=jnp.int32))
    new_state = accumulator + lax.optimization_barrier(jnp.mean(grads * grads, axis=-1))
    updated = touched_rows - learn_rate * grads / (jnp.sqrt(new_state)[..., None] + 1e-08)
    return (grads, updated)
```

```python
import functools

import jax
import jax.numpy as jnp
from jax import lax
from jax.experimental import pallas as pl
from jax.experimental.pallas import tpu as pltpu
from jax.sharding import PartitionSpec as P

learn_rate = 0.5
RELAYS = 4
MESH = pl.DeviceIdType.MESH


def loop(count, body):
    if count <= 8:
        for i in range(count):
            body(i)
    else:

        @pl.loop(0, count)
        def _(i):
            body(i)


def paired(me, i, count):
    if count & (count - 1):
        return lax.rem(me + i, count)
    out, bit = 0, 1
    while bit < count:
        a = (me // bit) % 2
        b = (i // bit) % 2
        out = out + bit * ((a + b) % 2)
        bit *= 2
    return out


def far_of(reps):
    return reps - 1 if reps > 2 else reps


def send_order(reps):
    if reps == 4:
        return ((2, 0, 1, 3), (0, 3, 2, 1), (0, 1, 3, 2), (0, 1, 2, 3))
    return tuple(
        tuple(range(z)) + tuple(range(reps - 1, z, -1)) + (z,) for z in range(reps)
    )


def tally_order(reps):
    return tuple(tuple(sorted(range(reps), key=lambda g: (abs(g - z), g))) for z in range(reps))


def add_order(reps):
    out = []
    for z, near in enumerate(tally_order(reps)):
        first = []
        if reps > 2 and z == 1:
            first.append(reps - 1)
        if reps > 2 and z == reps - 2:
            first.append(0)
        out.append(tuple(first) + tuple(g for g in near if g not in first))
    return tuple(out)


def pick(table, z, k):
    out = table[-1][k]
    for row in range(len(table) - 1):
        out = jnp.where(z == row, table[row][k], out)
    return out


def kernel(
    shards, reps,
    pooled, lengths, slots, weights,
    acc,
    pooled_v, staged, samples, ids_v, tally_v,
    load_sem, send_sem, recv_sem, hop_send, hop_recv, id_send, id_recv, here,
):
    me, z = lax.axis_index("shard"), lax.axis_index("rep")
    per = staged.shape[1]
    height, width = acc.shape
    count = samples.shape[1]
    entries = slots.shape[2]
    far = far_of(reps)
    relays = hop_recv.shape[0]
    group = shards // relays
    rows = group * per

    load_pooled = pltpu.make_async_copy(pooled, pooled_v, load_sem.at[0])
    load_ids = []
    for n, (own, at, size) in enumerate(
        ((slots, 0, entries), (weights, entries, entries), (lengths, 2 * entries, count))
    ):
        load_ids.append(
            pltpu.make_async_copy(
                own.at[0], ids_v.at[z, :, pl.ds(at, size)], load_sem.at[1 + n]
            )
        )
    load_pooled.start()
    for copy in load_ids:
        copy.start()

    barrier = pltpu.get_barrier_semaphore()

    def near(j):
        return (j - z < far) & (z - j < far)

    def greet(sem, j, i):
        pl.semaphore_signal(
            sem, inc=1, device_id={"shard": paired(me, i, shards), "rep": j}, device_id_type=MESH
        )

    for j in range(reps - 1, 0, -1):

        @pl.when(j > z)
        def _(j=j):
            greet(barrier, j, 0)

            @pl.when(near(j))
            def _():
                loop(shards - 1, lambda i: greet(barrier, j, i + 1))

    def greet_mates(sem, above):
        def one(i):
            p = paired(me, i + 1, shards)

            @pl.when((p > me) if above else (p < me))
            def _():
                greet(sem, z, i + 1)

        loop(shards - 1, one)

    greet_mates(barrier, True)
    below = me
    for j in range(reps - 1):
        below = below + jnp.where(j < z, jnp.where(near(j), shards, 1), 0)

    @pl.when(below > 0)
    def _():
        pl.semaphore_wait(barrier, below)

    for j in range(reps - 1):

        @pl.when(j < z)
        def _(j=j):
            greet(here.at[z], j, 0)

            @pl.when(near(j))
            def _():
                loop(shards - 1, lambda i: greet(here.at[z], j, i + 1))

    greet_mates(here.at[z], False)

    load_pooled.wait()

    def stage(t):
        staged[t] = pooled_v[:, 0, t, :]

    loop(shards, stage)
    for copy in load_ids:
        copy.wait()

    def id_copy(g, peer):
        return pltpu.make_async_remote_copy(
            src_ref=ids_v.at[g],
            dst_ref=ids_v.at[g],
            send_sem=id_send.at[peer],
            recv_sem=id_recv.at[g],
            device_id={"rep": peer},
            device_id_type=MESH,
        )

    def piece(g, src, j, dst):
        return pltpu.make_async_remote_copy(
            src_ref=staged.at[dst],
            dst_ref=samples.at[g, pl.ds(pl.multiple_of(src * per, per), per), :],
            send_sem=send_sem.at[j, dst],
            recv_sem=recv_sem.at[g, src],
            device_id={"shard": dst, "rep": j},
            device_id_type=MESH,
        )

    def hop(g, c, peer):
        part = samples.at[g, pl.ds(pl.multiple_of(c * rows, rows), rows), :]
        return pltpu.make_async_remote_copy(
            src_ref=part,
            dst_ref=part,
            send_sem=hop_send.at[peer, c],
            recv_sem=hop_recv.at[c],
            device_id={"rep": peer},
            device_id_type=MESH,
        )

    def each_piece(j, body):
        @pl.when(near(j))
        def _():
            def one(i):
                @pl.when((j != z) | (i != me))
                def _():
                    body(i)

            loop(shards, one)

    order = send_order(reps)
    for k in range(reps):
        j = pick(order, z, k)

        @pl.when(j > z)
        def _():
            pl.semaphore_wait(here.at[j], jnp.where(near(j), shards, 1))

        @pl.when((j == z) & (me < shards - 1))
        def _():
            pl.semaphore_wait(here.at[j], shards - 1 - me)

        @pl.when(j != z)
        def _():
            id_copy(z, j).start()

        each_piece(j, lambda p: piece(z, me, j, p).start())

    samples[z, pl.ds(pl.multiple_of(me * per, per), per), :] = staged[me]

    def tally(g):
        span = min(512, entries)
        lens = ids_v[g, :, pl.ds(2 * entries, count)].astype(jnp.float32)
        ii = lax.broadcasted_iota(jnp.int32, (count, count), 0)
        jj = lax.broadcasted_iota(jnp.int32, (count, count), 1)
        ends = jnp.sum(jnp.where(jj <= ii, lens, 0.0), axis=1, keepdims=True).astype(jnp.int32)
        starts = jnp.sum(jnp.where(jj < ii, lens, 0.0), axis=1, keepdims=True).astype(jnp.int32)

        def block(b, total):
            at = pl.multiple_of(b * span, span)
            target = ids_v[g, :, pl.ds(at, span)]
            factor = ids_v[g, :, pl.ds(entries + at, span)].astype(jnp.float32) * 0.0625
            pos = at + lax.broadcasted_iota(jnp.int32, (1, span), 1)
            within = (pos >= starts) & (pos < ends)
            member = jnp.where(within, 1.0, 0.0).astype(jnp.bfloat16)
            ids = lax.broadcasted_iota(jnp.int32, (height, span), 0)
            chosen = jnp.where(ids == target, factor, 0.0).astype(jnp.bfloat16)
            return total + lax.dot_general(
                chosen, member, (((1,), (1,)), ((), ())), preferred_element_type=jnp.float32
            )

        total = lax.fori_loop(
            0, entries // span, block, jnp.zeros((height, count), jnp.float32)
        )
        high = total.astype(jnp.bfloat16)
        low = (total - high.astype(jnp.float32)).astype(jnp.bfloat16)
        tally_v[g, :, :count] = high
        tally_v[g, :, count:] = low

    @pl.loop(0, reps)
    def _(k):
        g = z
        for step in range(1, reps):
            g = jnp.where(k == step, pick(tally_order(reps), z, step), g)

        @pl.when(g != z)
        def _():
            id_copy(g, g).wait_recv()

        tally(g)

    def relay_to(g):
        down = (z == 1) & (g == reps - 1)
        up = (z == reps - 2) & (g == 0)
        return (down | up) if reps > 2 else False, jnp.where(down, 0, reps - 1)

    def arrive(g):
        relay, peer = relay_to(g)

        def part(c):
            def one(q):
                src = c * group + q

                @pl.when((g != z) | (src != me))
                def _():
                    piece(g, src, z, src).wait_recv()

            loop(group, one)
            if reps > 2:

                @pl.when(relay)
                def _():
                    hop(g, c, peer).start()

        @pl.when(near(g))
        def _():
            loop(relays, part)

        if reps > 2:

            @pl.when(jnp.logical_not(near(g)))
            def _():
                loop(relays, lambda c: hop(g, c, g).wait_recv())

    def add(g, first):
        rest = samples[g]
        total = None
        for _ in range(2):
            part = rest.astype(jnp.bfloat16)
            rest = rest - part.astype(jnp.float32)
            term = jnp.dot(
                tally_v[g],
                jnp.concatenate([part, part], axis=0),
                preferred_element_type=jnp.float32,
            )
            total = term if total is None else total + term
        if first:
            acc[...] = total
        else:
            acc[...] += total

    order = add_order(reps)
    for k in range(reps):
        g = pick(order, z, k)
        arrive(g)
        add(g, k == 0)

    for j in range(reps):
        each_piece(j, lambda p: piece(z, me, j, p).wait_send())

        @pl.when(j != z)
        def _(j=j):
            id_copy(z, j).wait_send()

    if reps > 2:
        for g, at, peer in ((reps - 1, 1, 0), (0, reps - 2, reps - 1)):

            @pl.when(z == at)
            def _(g=g, peer=peer):
                loop(relays, lambda c: hop(g, c, peer).wait_send())


def finish(reps, acc, touched, state, grad_out, rows_out):
    z = lax.axis_index("rep")
    height, width = acc.shape
    part = height // reps
    grad_out[0] = acc[pl.ds(pl.multiple_of(z * part, part), part), :]
    block = min(128, height)
    ii = lax.broadcasted_iota(jnp.int32, (block, block), 0)
    jj = lax.broadcasted_iota(jnp.int32, (block, block), 1)
    for b in range(height // block):
        at = slice(b * block, (b + 1) * block)
        grads = acc[at, :]
        old = jnp.sum(jnp.where(ii == jj, state[:, at], 0.0), axis=1, keepdims=True)
        new = old + jnp.sum(grads * grads, axis=1, keepdims=True) * (1.0 / width)
        rows_out[0, at, :] = touched[0, at, :] - grads * (learn_rate / (jnp.sqrt(new) + 1e-08))


def per_device(pooled_grad, bag_lengths, row_slots, id_weights, touched_rows, accumulator):
    shards, reps = lax.axis_size("shard"), lax.axis_size("rep")
    per, _, tables, width = pooled_grad.shape
    height = touched_rows.shape[1]
    entries = row_slots.shape[2]
    count = per * shards
    relays = min(RELAYS, shards)
    vmem = pl.BlockSpec(memory_space=pltpu.VMEM)
    hbm = pl.BlockSpec(memory_space=pltpu.HBM)
    dma = pltpu.SemaphoreType.DMA
    sent = [
        pltpu.with_memory_space_constraint(x, pltpu.HBM)
        for x in (pooled_grad, bag_lengths, row_slots, id_weights)
    ]
    total = pl.pallas_call(
        functools.partial(kernel, shards, reps),
        out_shape=jax.ShapeDtypeStruct((height, width), jnp.float32),
        in_specs=[hbm] * 4,
        out_specs=vmem,
        scratch_shapes=[
            pltpu.VMEM((per, 1, tables, width), jnp.float32),
            pltpu.VMEM((tables, per, width), jnp.float32),
            pltpu.VMEM((reps, count, width), jnp.float32),
            pltpu.VMEM((reps, 1, 2 * entries + count), jnp.int32),
            pltpu.VMEM((reps, height, 2 * count), jnp.bfloat16),
            dma((4,)),
            dma((reps, shards)),
            dma((reps, shards)),
            dma((reps, relays)),
            dma((relays,)),
            dma((reps,)),
            dma((reps,)),
            pltpu.SemaphoreType.REGULAR((reps,)),
        ],
        compiler_params=pltpu.CompilerParams(
            collective_id=0, has_side_effects=True, vmem_limit_bytes=40 * 1024 * 1024
        ),
    )(*sent)
    return pl.pallas_call(
        functools.partial(finish, reps),
        out_shape=(
            jax.ShapeDtypeStruct((1, height // reps, width), jnp.float32),
            jax.ShapeDtypeStruct((1, height, width), jnp.float32),
        ),
        in_specs=[vmem] * 3,
        out_specs=(vmem, vmem),
        compiler_params=pltpu.CompilerParams(vmem_limit_bytes=16 * 1024 * 1024),
    )(total, touched_rows, accumulator)


def solution(mesh):
    placed = (
        P("shard", "rep", None, None),
        P("shard", "rep", None),
        P("shard", "rep", None),
        P("shard", "rep", None),
        P("shard", None, None),
        P("shard", None),
    )
    return jax.shard_map(
        per_device,
        mesh=mesh,
        in_specs=placed,
        out_specs=(P("shard", "rep", None), P("shard", None, None)),
        check_vma=False,
    )
```

```python
import functools

import jax
import jax.numpy as jnp
from jax import lax
from jax.experimental import pallas as pl
from jax.experimental.pallas import tpu as pltpu
from jax.sharding import PartitionSpec as P

learn_rate = 0.5
RELAYS = 4
MESH = pl.DeviceIdType.MESH


def loop(count, body):
    if count <= 8:
        for i in range(count):
            body(i)
    else:

        @pl.loop(0, count)
        def _(i):
            body(i)


def paired(me, i, count):
    if count & (count - 1):
        return lax.rem(me + i, count)
    out, bit = 0, 1
    while bit < count:
        a = (me // bit) % 2
        b = (i // bit) % 2
        out = out + bit * ((a + b) % 2)
        bit *= 2
    return out


def far_of(reps):
    return reps - 1 if reps > 2 else reps


def plan(reps):
    if reps == 4:
        rows = (
            "T0 P0 I1 I2 P2 I3 P1 T1 T2 T3 W0 A0 W1 A1 W2 A2 W3 A3",
            "I0 P0 T1 I2 I3 P3 P2 P1 T0 T2 T3 W3 A3 W1 A1 W0 A0 W2 A2",
            "I0 I1 P0 P1 T2 I3 P3 P2 T1 T3 T0 W0 A0 W2 A2 W1 A1 W3 A3",
            "I2 I1 I0 P1 P2 T3 P3 T2 T1 T0 W3 A3 W2 A2 W1 A1 W0 A0",
        )
        steps = [[(s[0], int(s[1:])) for s in row.split()] for row in rows]
    else:
        steps = []
        for z in range(reps):
            low, high = list(range(z)), list(range(z + 1, reps))
            near = sorted(range(reps), key=lambda g: (abs(g - z), g))
            first = []
            if reps > 2 and z == 1:
                first.append(reps - 1)
            if reps > 2 and z == reps - 2:
                first.append(0)
            row = [("I", j) for j in low] + [("P", j) for j in low + [z]]
            row += [("I", j) for j in high] + [("P", j) for j in high]
            row += [("T", g) for g in near]
            for g in first + [g for g in near if g not in first]:
                row += [("W", g), ("A", g)]
            steps.append(row)
    longest = max(len(row) for row in steps)
    kinds = [["IPTWA".index(s[0]) for s in row] + [5] * (longest - len(row)) for row in steps]
    planes = [[s[1] for s in row] + [0] * (longest - len(row)) for row in steps]
    return kinds, planes


def pick(table, z, k):
    out = 0
    for row in range(len(table)):
        for col in range(len(table[row])):
            if table[row][col]:
                out = jnp.where((z == row) & (k == col), table[row][col], out)
    return out


def kernel(
    shards, reps,
    pooled, lengths, slots, weights,
    acc,
    pooled_v, staged, samples, ids_v, tally_v,
    load_sem, send_sem, recv_sem, hop_send, hop_recv, id_send, id_recv, here,
):
    me, z = lax.axis_index("shard"), lax.axis_index("rep")
    per = staged.shape[1]
    height, width = acc.shape
    count = samples.shape[1]
    entries = slots.shape[2]
    far = far_of(reps)
    relays = hop_recv.shape[0]
    group = shards // relays
    rows = group * per

    load_pooled = pltpu.make_async_copy(pooled, pooled_v, load_sem.at[0])
    load_ids = []
    for n, (own, at, size) in enumerate(
        ((slots, 0, entries), (weights, entries, entries), (lengths, 2 * entries, count))
    ):
        load_ids.append(
            pltpu.make_async_copy(
                own.at[0], ids_v.at[z, :, pl.ds(at, size)], load_sem.at[1 + n]
            )
        )
    load_pooled.start()
    for copy in load_ids:
        copy.start()

    barrier = pltpu.get_barrier_semaphore()

    def near(j):
        return (j - z < far) & (z - j < far)

    def greet(sem, j, i):
        pl.semaphore_signal(
            sem, inc=1, device_id={"shard": paired(me, i, shards), "rep": j}, device_id_type=MESH
        )

    for j in range(reps - 1, 0, -1):

        @pl.when(j > z)
        def _(j=j):
            greet(barrier, j, 0)

            @pl.when(near(j))
            def _():
                loop(shards - 1, lambda i: greet(barrier, j, i + 1))

    def greet_mates(sem, above):
        def one(i):
            p = paired(me, i + 1, shards)

            @pl.when((p > me) if above else (p < me))
            def _():
                greet(sem, z, i + 1)

        loop(shards - 1, one)

    greet_mates(barrier, True)
    below = me
    for j in range(reps - 1):
        below = below + jnp.where(j < z, jnp.where(near(j), shards, 1), 0)

    @pl.when(below > 0)
    def _():
        pl.semaphore_wait(barrier, below)

    for j in range(reps - 1):

        @pl.when(j < z)
        def _(j=j):
            greet(here.at[z], j, 0)

            @pl.when(near(j))
            def _():
                loop(shards - 1, lambda i: greet(here.at[z], j, i + 1))

    greet_mates(here.at[z], False)

    load_pooled.wait()

    def stage(t):
        staged[t] = pooled_v[:, 0, t, :]

    loop(shards, stage)
    for copy in load_ids:
        copy.wait()

    def id_copy(g, peer):
        return pltpu.make_async_remote_copy(
            src_ref=ids_v.at[g],
            dst_ref=ids_v.at[g],
            send_sem=id_send.at[peer],
            recv_sem=id_recv.at[g],
            device_id={"rep": peer},
            device_id_type=MESH,
        )

    def piece(g, src, j, dst):
        return pltpu.make_async_remote_copy(
            src_ref=staged.at[dst],
            dst_ref=samples.at[g, pl.ds(pl.multiple_of(src * per, per), per), :],
            send_sem=send_sem.at[j, dst],
            recv_sem=recv_sem.at[g, src],
            device_id={"shard": dst, "rep": j},
            device_id_type=MESH,
        )

    def hop(g, c, peer):
        part = samples.at[g, pl.ds(pl.multiple_of(c * rows, rows), rows), :]
        return pltpu.make_async_remote_copy(
            src_ref=part,
            dst_ref=part,
            send_sem=hop_send.at[peer, c],
            recv_sem=hop_recv.at[c],
            device_id={"rep": peer},
            device_id_type=MESH,
        )

    def each_piece(j, body):
        @pl.when(near(j))
        def _():
            def one(i):
                @pl.when((j != z) | (i != me))
                def _():
                    body(i)

            loop(shards, one)

    def send_ids(j):
        @pl.when(j > z)
        def _():
            pl.semaphore_wait(here.at[j], jnp.where(near(j), shards, 1))

        id_copy(z, j).start()

    def send_pieces(j):
        @pl.when((j == z) & (me < shards - 1))
        def _():
            pl.semaphore_wait(here.at[j], shards - 1 - me)

        each_piece(j, lambda p: piece(z, me, j, p).start())

    samples[z, pl.ds(pl.multiple_of(me * per, per), per), :] = staged[me]
    acc[...] = jnp.zeros_like(acc)

    def tally(g):
        @pl.when(g != z)
        def _():
            id_copy(g, g).wait_recv()

        span = min(512, entries)
        lens = ids_v[g, :, pl.ds(2 * entries, count)].astype(jnp.float32)
        ii = lax.broadcasted_iota(jnp.int32, (count, count), 0)
        jj = lax.broadcasted_iota(jnp.int32, (count, count), 1)
        ends = jnp.sum(jnp.where(jj <= ii, lens, 0.0), axis=1, keepdims=True).astype(jnp.int32)
        starts = jnp.sum(jnp.where(jj < ii, lens, 0.0), axis=1, keepdims=True).astype(jnp.int32)
        starts = jnp.broadcast_to(starts, (count, span)).astype(jnp.int16)
        ends = jnp.broadcast_to(ends, (count, span)).astype(jnp.int16)
        ids = lax.broadcasted_iota(jnp.int16, (height, span), 0)

        def rows_of(x, rows, dtype):
            return jnp.concatenate([jnp.broadcast_to(x, (16, span)).astype(dtype)] * (rows // 16), 0)

        def block(b, total):
            at = pl.multiple_of(b * span, span)
            target = rows_of(ids_v[g, :, pl.ds(at, span)], height, jnp.int16)
            factor = ids_v[g, :, pl.ds(entries + at, span)].astype(jnp.float32) * 0.0625
            factor = rows_of(factor, height, jnp.bfloat16)
            pos = rows_of(at + lax.broadcasted_iota(jnp.int32, (1, span), 1), count, jnp.int16)
            one, none = jnp.bfloat16(1), jnp.bfloat16(0)
            member = jnp.where((pos >= starts) & (pos < ends), one, none)
            chosen = jnp.where(ids == target, factor, none)
            return total + lax.dot_general(
                chosen, member, (((1,), (1,)), ((), ())), preferred_element_type=jnp.float32
            )

        total = jnp.zeros((height, count), jnp.float32)
        if entries // span <= 4:
            for b in range(entries // span):
                total = block(b, total)
        else:
            total = lax.fori_loop(0, entries // span, block, total)
        high = total.astype(jnp.bfloat16)
        low = (total - high.astype(jnp.float32)).astype(jnp.bfloat16)
        tally_v[g, :, :count] = high
        tally_v[g, :, count:] = low

    def relay_to(g):
        down = (z == 1) & (g == reps - 1)
        up = (z == reps - 2) & (g == 0)
        return (down | up) if reps > 2 else False, jnp.where(down, 0, reps - 1)

    def arrive(g):
        relay, peer = relay_to(g)

        def part(c):
            def one(q):
                src = c * group + q

                @pl.when((g != z) | (src != me))
                def _():
                    piece(g, src, z, src).wait_recv()

            loop(group, one)
            if reps > 2:

                @pl.when(relay)
                def _():
                    hop(g, c, peer).start()

        @pl.when(near(g))
        def _():
            loop(relays, part)

        if reps > 2:

            @pl.when(jnp.logical_not(near(g)))
            def _():
                loop(relays, lambda c: hop(g, c, g).wait_recv())

    def add(g):
        rest = samples[g]
        total = None
        for _ in range(2):
            part = rest.astype(jnp.bfloat16)
            rest = rest - part.astype(jnp.float32)
            term = jnp.dot(
                tally_v[g],
                jnp.concatenate([part, part], axis=0),
                preferred_element_type=jnp.float32,
            )
            total = term if total is None else total + term
        acc[...] += total

    kinds, planes = plan(reps)

    @pl.loop(0, len(kinds[0]))
    def _(k):
        kind, j = pick(kinds, z, k), pick(planes, z, k)
        for at, act in enumerate((send_ids, send_pieces, tally, arrive, add)):

            @pl.when(kind == at)
            def _(act=act):
                act(j)

    for j in range(reps):
        each_piece(j, lambda p: piece(z, me, j, p).wait_send())

        @pl.when(j != z)
        def _(j=j):
            id_copy(z, j).wait_send()

    if reps > 2:
        for g, at, peer in ((reps - 1, 1, 0), (0, reps - 2, reps - 1)):

            @pl.when(z == at)
            def _(g=g, peer=peer):
                loop(relays, lambda c: hop(g, c, peer).wait_send())


def finish(reps, acc, touched, state, grad_out, rows_out):
    z = lax.axis_index("rep")
    height, width = acc.shape
    part = height // reps
    grad_out[0] = acc[pl.ds(pl.multiple_of(z * part, part), part), :]
    block = min(128, height)
    ii = lax.broadcasted_iota(jnp.int32, (block, block), 0)
    jj = lax.broadcasted_iota(jnp.int32, (block, block), 1)
    for b in range(height // block):
        at = slice(b * block, (b + 1) * block)
        grads = acc[at, :]
        old = jnp.sum(jnp.where(ii == jj, state[:, at], 0.0), axis=1, keepdims=True)
        new = old + jnp.sum(grads * grads, axis=1, keepdims=True) * (1.0 / width)
        rows_out[0, at, :] = touched[0, at, :] - grads * (learn_rate / (jnp.sqrt(new) + 1e-08))


def per_device(pooled_grad, bag_lengths, row_slots, id_weights, touched_rows, accumulator):
    shards, reps = lax.axis_size("shard"), lax.axis_size("rep")
    per, _, tables, width = pooled_grad.shape
    height = touched_rows.shape[1]
    entries = row_slots.shape[2]
    count = per * shards
    relays = min(RELAYS, shards)
    vmem = pl.BlockSpec(memory_space=pltpu.VMEM)
    hbm = pl.BlockSpec(memory_space=pltpu.HBM)
    dma = pltpu.SemaphoreType.DMA
    sent = [
        pltpu.with_memory_space_constraint(x, pltpu.HBM)
        for x in (pooled_grad, bag_lengths, row_slots, id_weights)
    ]
    total = pl.pallas_call(
        functools.partial(kernel, shards, reps),
        out_shape=jax.ShapeDtypeStruct((height, width), jnp.float32),
        in_specs=[hbm] * 4,
        out_specs=vmem,
        scratch_shapes=[
            pltpu.VMEM((per, 1, tables, width), jnp.float32),
            pltpu.VMEM((tables, per, width), jnp.float32),
            pltpu.VMEM((reps, count, width), jnp.float32),
            pltpu.VMEM((reps, 1, 2 * entries + count), jnp.int32),
            pltpu.VMEM((reps, height, 2 * count), jnp.bfloat16),
            dma((4,)),
            dma((reps, shards)),
            dma((reps, shards)),
            dma((reps, relays)),
            dma((relays,)),
            dma((reps,)),
            dma((reps,)),
            pltpu.SemaphoreType.REGULAR((reps,)),
        ],
        compiler_params=pltpu.CompilerParams(
            collective_id=0, has_side_effects=True, vmem_limit_bytes=40 * 1024 * 1024
        ),
    )(*sent)
    return pl.pallas_call(
        functools.partial(finish, reps),
        out_shape=(
            jax.ShapeDtypeStruct((1, height // reps, width), jnp.float32),
            jax.ShapeDtypeStruct((1, height, width), jnp.float32),
        ),
        in_specs=[vmem] * 3,
        out_specs=(vmem, vmem),
        compiler_params=pltpu.CompilerParams(vmem_limit_bytes=16 * 1024 * 1024),
    )(total, touched_rows, accumulator)


def solution(mesh):
    placed = (
        P("shard", "rep", None, None),
        P("shard", "rep", None),
        P("shard", "rep", None),
        P("shard", "rep", None),
        P("shard", None, None),
        P("shard", None),
    )
    return jax.shard_map(
        per_device,
        mesh=mesh,
        in_specs=placed,
        out_specs=(P("shard", "rep", None), P("shard", None, None)),
        check_vma=False,
    )
```

```python
import functools

import jax
import jax.numpy as jnp
from jax import lax
from jax.experimental import pallas as pl
from jax.experimental.pallas import tpu as pltpu
from jax.sharding import PartitionSpec as P

learn_rate = 0.5
RELAYS = 4
KINDS = "IPTWA"
MESH = pl.DeviceIdType.MESH


def loop(count, body):
    if count <= 8:
        for i in range(count):
            body(i)
    else:

        @pl.loop(0, count)
        def _(i):
            body(i)


def paired(me, i, count):
    if count & (count - 1):
        return lax.rem(me + i, count)
    out, bit = 0, 1
    while bit < count:
        a = (me // bit) % 2
        b = (i // bit) % 2
        out = out + bit * ((a + b) % 2)
        bit *= 2
    return out


def far_of(reps):
    return reps - 1 if reps > 2 else reps


def plan(reps):
    def send(j):
        return ("P", j)

    def ids(j):
        return ("I", j)

    def weigh(g):
        return ("T", g)

    def take(g):
        return ("W", g), ("A", g)

    if reps == 4:
        steps = [
            [weigh(0), send(0), ids(1), ids(2), send(2), ids(3), send(1), ('W',0), ('A',0), weigh(1), ('W',1), ('A',1), weigh(2), ('W',2), ('A',2), weigh(3), ('W',3), ('A',3)],
            [ids(0), send(0), weigh(1), ids(2), ids(3), send(3), send(2), send(1), ('W',3), weigh(0), weigh(2), weigh(3), ('A',3), ('W',1), ('A',1), ('W',0), ('A',0), ('W',2), ('A',2)],
            [ids(0), ids(1), send(0), send(1), weigh(2), ids(3), send(3), send(2), ('W',0), weigh(1), weigh(3), weigh(0), ('A',0), ('W',2), ('A',2), ('W',3), ('A',3), ('W',1), ('A',1)],
            [ids(2), ids(1), ids(0), send(1), send(2), weigh(3), send(3), weigh(2), weigh(1), weigh(0), ('W',2), ('A',2), ('W',1), ('A',1), ('W',3), ('A',3), ('W',0), ('A',0)],
        ]
    else:
        steps = []
        for z in range(reps):
            low, high = range(z), range(z + 1, reps)
            near = sorted(range(reps), key=lambda g: (abs(g - z), g))
            relayed = [g for g, at in ((reps - 1, 1), (0, reps - 2)) if reps > 2 and z == at]
            row = [ids(j) for j in low] + [send(j) for j in [*low, z]]
            row += [ids(j) for j in high] + [send(j) for j in high]
            row += [weigh(g) for g in near]
            for g in relayed + [g for g in near if g not in relayed]:
                row += take(g)
            steps.append(row)
    longest = max(len(row) for row in steps)
    rows = []
    for row in steps:
        codes = [KINDS.index(kind) * reps + j for kind, j in row]
        codes += [len(KINDS) * reps] * (longest - len(row))
        base = 1
        while base <= len(KINDS) * reps:
            base *= 2
        held = 1
        while base ** (held + 1) < 2**31:
            held += 1
        words = []
        for at in range(0, longest, held):
            words.append(sum(c * base**n for n, c in enumerate(codes[at : at + held])))
        rows.append(words)
    return longest, base, held, rows


def kernel(
    shards, reps,
    pooled, lengths, slots, weights,
    acc,
    pooled_v, staged, samples, ids_v, tally_v,
    load_sem, send_sem, recv_sem, hop_send, hop_recv, id_send, id_recv, here,
):
    me, z = lax.axis_index("shard"), lax.axis_index("rep")
    per = staged.shape[1]
    height, width = acc.shape
    count = samples.shape[1]
    entries = slots.shape[2]
    far = far_of(reps)
    relays = hop_recv.shape[0]
    group = shards // relays
    rows = group * per

    load_pooled = pltpu.make_async_copy(pooled, pooled_v, load_sem.at[0])
    load_ids = []
    for n, (own, at, size) in enumerate(
        ((slots, 0, entries), (weights, entries, entries), (lengths, 2 * entries, count))
    ):
        load_ids.append(
            pltpu.make_async_copy(
                own.at[0], ids_v.at[z, :, pl.ds(at, size)], load_sem.at[1 + n]
            )
        )
    load_pooled.start()
    for copy in load_ids:
        copy.start()

    barrier = pltpu.get_barrier_semaphore()

    def near(j):
        return (j - z < far) & (z - j < far)

    def greet(sem, j, i):
        pl.semaphore_signal(
            sem, inc=1, device_id={"shard": paired(me, i, shards), "rep": j}, device_id_type=MESH
        )

    for j in range(reps - 1, 0, -1):

        @pl.when(j > z)
        def _(j=j):
            greet(barrier, j, 0)

            @pl.when(near(j))
            def _():
                loop(shards - 1, lambda i: greet(barrier, j, i + 1))

    def greet_mates(sem, above):
        def one(i):
            p = paired(me, i + 1, shards)

            @pl.when((p > me) if above else (p < me))
            def _():
                greet(sem, z, i + 1)

        loop(shards - 1, one)

    greet_mates(barrier, True)
    below = me
    for j in range(reps - 1):
        below = below + jnp.where(j < z, jnp.where(near(j), shards, 1), 0)

    @pl.when(below > 0)
    def _():
        pl.semaphore_wait(barrier, below)

    for j in range(reps - 1):

        @pl.when(j < z)
        def _(j=j):
            greet(here.at[z], j, 0)

            @pl.when(near(j))
            def _():
                loop(shards - 1, lambda i: greet(here.at[z], j, i + 1))

    greet_mates(here.at[z], False)

    load_pooled.wait()

    def stage(t):
        staged[t] = pooled_v[:, 0, t, :]

    loop(shards, stage)
    for copy in load_ids:
        copy.wait()

    def id_copy(g, peer):
        return pltpu.make_async_remote_copy(
            src_ref=ids_v.at[g],
            dst_ref=ids_v.at[g],
            send_sem=id_send.at[peer],
            recv_sem=id_recv.at[g],
            device_id={"rep": peer},
            device_id_type=MESH,
        )

    def piece(g, src, j, dst):
        return pltpu.make_async_remote_copy(
            src_ref=staged.at[dst],
            dst_ref=samples.at[g, pl.ds(pl.multiple_of(src * per, per), per), :],
            send_sem=send_sem.at[j, dst],
            recv_sem=recv_sem.at[g, src],
            device_id={"shard": dst, "rep": j},
            device_id_type=MESH,
        )

    def hop(g, c, peer):
        part = samples.at[g, pl.ds(pl.multiple_of(c * rows, rows), rows), :]
        return pltpu.make_async_remote_copy(
            src_ref=part,
            dst_ref=part,
            send_sem=hop_send.at[peer, c],
            recv_sem=hop_recv.at[c],
            device_id={"rep": peer},
            device_id_type=MESH,
        )

    def each_piece(j, body):
        @pl.when(near(j))
        def _():
            def one(i):
                body(paired(me, shards - 1 - i, shards))

            loop(shards - 1, one)

            @pl.when(j != z)
            def _():
                body(me)

    def send_ids(j):
        @pl.when(j > z)
        def _():
            pl.semaphore_wait(here.at[j], jnp.where(near(j), shards, 1))

        id_copy(z, j).start()

    def send_pieces(j):
        @pl.when((j == z) & (me < shards - 1))
        def _():
            pl.semaphore_wait(here.at[j], shards - 1 - me)

        each_piece(j, lambda p: piece(z, me, j, p).start())

    samples[z, pl.ds(pl.multiple_of(me * per, per), per), :] = staged[me]
    acc[...] = jnp.zeros_like(acc)

    def tally(g):
        @pl.when(g != z)
        def _():
            id_copy(g, g).wait_recv()

        span = min(512, entries)
        lens = ids_v[g, :, pl.ds(2 * entries, count)].astype(jnp.float32)
        ii = lax.broadcasted_iota(jnp.int32, (count, count), 0)
        jj = lax.broadcasted_iota(jnp.int32, (count, count), 1)
        ends = jnp.sum(jnp.where(jj <= ii, lens, 0.0), axis=1, keepdims=True).astype(jnp.int32)
        starts = jnp.sum(jnp.where(jj < ii, lens, 0.0), axis=1, keepdims=True).astype(jnp.int32)
        starts = jnp.broadcast_to(starts, (count, span)).astype(jnp.int16)
        ends = jnp.broadcast_to(ends, (count, span)).astype(jnp.int16)
        ids = lax.broadcasted_iota(jnp.int16, (height, span), 0)

        def rows_of(x, rows, dtype):
            return jnp.concatenate([jnp.broadcast_to(x, (16, span)).astype(dtype)] * (rows // 16), 0)

        def block(b, total):
            at = pl.multiple_of(b * span, span)
            target = rows_of(ids_v[g, :, pl.ds(at, span)], height, jnp.int16)
            factor = ids_v[g, :, pl.ds(entries + at, span)].astype(jnp.float32) * 0.0625
            factor = rows_of(factor, height, jnp.bfloat16)
            pos = rows_of(at + lax.broadcasted_iota(jnp.int32, (1, span), 1), count, jnp.int16)
            one, none = jnp.bfloat16(1), jnp.bfloat16(0)
            member = jnp.where((pos >= starts) & (pos < ends), one, none)
            chosen = jnp.where(ids == target, factor, none)
            return total + lax.dot_general(
                chosen, member, (((1,), (1,)), ((), ())), preferred_element_type=jnp.float32
            )

        total = jnp.zeros((height, count), jnp.float32)
        if entries // span <= 4:
            for b in range(entries // span):
                total = block(b, total)
        else:
            total = lax.fori_loop(0, entries // span, block, total)
        high = total.astype(jnp.bfloat16)
        low = (total - high.astype(jnp.float32)).astype(jnp.bfloat16)
        tally_v[g, :, :count] = high
        tally_v[g, :, count:] = low

    def relay_to(g):
        down = (z == 1) & (g == reps - 1)
        up = (z == reps - 2) & (g == 0)
        return (down | up) if reps > 2 else False, jnp.where(down, 0, reps - 1)

    def arrive(g):
        relay, peer = relay_to(g)

        def part(i):
            c = paired(me // group, relays - 1 - i, relays)

            def one(q):
                src = c * group + q

                @pl.when((g != z) | (src != me))
                def _():
                    piece(g, src, z, src).wait_recv()

            loop(group, one)
            if reps > 2:

                @pl.when(relay)
                def _():
                    hop(g, c, peer).start()

        @pl.when(near(g))
        def _():
            loop(relays, part)

        if reps > 2:

            @pl.when(jnp.logical_not(near(g)))
            def _():
                loop(relays, lambda c: hop(g, c, g).wait_recv())

    def add(g):
        rest = samples[g]
        total = None
        for _ in range(2):
            part = rest.astype(jnp.bfloat16)
            rest = rest - part.astype(jnp.float32)
            term = jnp.dot(
                tally_v[g],
                jnp.concatenate([part, part], axis=0),
                preferred_element_type=jnp.float32,
            )
            total = term if total is None else total + term
        acc[...] += total

    longest, base, held, rows_of_steps = plan(reps)
    words = []
    for n in range(len(rows_of_steps[0])):
        word = rows_of_steps[0][n]
        for row in range(1, reps):
            word = jnp.where(z == row, rows_of_steps[row][n], word)
        words.append(jnp.int32(word))

    def step(k, words):
        code = lax.rem(words[0], base)
        kind, j = lax.div(code, reps), lax.rem(code, reps)
        for at, act in enumerate((send_ids, send_pieces, tally, arrive, add)):

            @pl.when(kind == at)
            def _(act=act):
                act(j)

        over = lax.rem(k, held) == held - 1
        rest = (lax.div(words[0], base),) + tuple(words[1:])
        moved = tuple(words[1:]) + (words[0],)
        return tuple(jnp.where(over, b, a) for a, b in zip(rest, moved))

    lax.fori_loop(0, longest, step, tuple(words))

    for j in range(reps):
        each_piece(j, lambda p: piece(z, me, j, p).wait_send())

        @pl.when(j != z)
        def _(j=j):
            id_copy(z, j).wait_send()

    if reps > 2:
        for g, at, peer in ((reps - 1, 1, 0), (0, reps - 2, reps - 1)):

            @pl.when(z == at)
            def _(g=g, peer=peer):
                loop(relays, lambda c: hop(g, c, peer).wait_send())


def finish(reps, acc, touched, state, grad_out, rows_out, rows_v, sems):
    z = lax.axis_index("rep")
    height, width = acc.shape
    part = height // reps
    own = acc.at[pl.ds(pl.multiple_of(z * part, part), part), :]
    copies = [pltpu.make_async_copy(own, grad_out.at[0], sems.at[0])]
    copies[0].start()
    block = min(128, height)
    ii = lax.broadcasted_iota(jnp.int32, (block, block), 0)
    jj = lax.broadcasted_iota(jnp.int32, (block, block), 1)
    for b in range(height // block):
        at = slice(b * block, (b + 1) * block)
        grads = acc[at, :]
        old = jnp.sum(jnp.where(ii == jj, state[:, at], 0.0), axis=1, keepdims=True)
        new = old + jnp.sum(grads * grads, axis=1, keepdims=True) * (1.0 / width)
        rows_v[at, :] = touched[0, at, :] - grads * (learn_rate / (jnp.sqrt(new) + 1e-08))
        to = rows_out.at[0, pl.ds(b * block, block), :]
        copy = pltpu.make_async_copy(rows_v.at[pl.ds(b * block, block), :], to, sems.at[1 + b])
        copy.start()
        copies.append(copy)
    for copy in copies:
        copy.wait()


def per_device(pooled_grad, bag_lengths, row_slots, id_weights, touched_rows, accumulator):
    shards, reps = lax.axis_size("shard"), lax.axis_size("rep")
    per, _, tables, width = pooled_grad.shape
    height = touched_rows.shape[1]
    entries = row_slots.shape[2]
    count = per * shards
    relays = min(RELAYS, shards)
    vmem = pl.BlockSpec(memory_space=pltpu.VMEM)
    hbm = pl.BlockSpec(memory_space=pltpu.HBM)
    dma = pltpu.SemaphoreType.DMA
    sent = [
        pltpu.with_memory_space_constraint(x, pltpu.HBM)
        for x in (pooled_grad, bag_lengths, row_slots, id_weights)
    ]
    total = pl.pallas_call(
        functools.partial(kernel, shards, reps),
        out_shape=jax.ShapeDtypeStruct((height, width), jnp.float32),
        in_specs=[hbm] * 4,
        out_specs=vmem,
        scratch_shapes=[
            pltpu.VMEM((per, 1, tables, width), jnp.float32),
            pltpu.VMEM((tables, per, width), jnp.float32),
            pltpu.VMEM((reps, count, width), jnp.float32),
            pltpu.VMEM((reps, 1, 2 * entries + count), jnp.int32),
            pltpu.VMEM((reps, height, 2 * count), jnp.bfloat16),
            dma((4,)),
            dma((reps, shards)),
            dma((reps, shards)),
            dma((reps, relays)),
            dma((relays,)),
            dma((reps,)),
            dma((reps,)),
            pltpu.SemaphoreType.REGULAR((reps,)),
        ],
        compiler_params=pltpu.CompilerParams(
            collective_id=0, has_side_effects=True, vmem_limit_bytes=40 * 1024 * 1024
        ),
    )(*sent)
    return pl.pallas_call(
        functools.partial(finish, reps),
        out_shape=(
            jax.ShapeDtypeStruct((1, height // reps, width), jnp.float32),
            jax.ShapeDtypeStruct((1, height, width), jnp.float32),
        ),
        in_specs=[vmem] * 3,
        out_specs=(hbm, hbm),
        scratch_shapes=[
            pltpu.VMEM((height, width), jnp.float32),
            dma((1 + height // min(128, height),)),
        ],
        compiler_params=pltpu.CompilerParams(vmem_limit_bytes=16 * 1024 * 1024),
    )(total, touched_rows, accumulator)


def solution(mesh):
    placed = (
        P("shard", "rep", None, None),
        P("shard", "rep", None),
        P("shard", "rep", None),
        P("shard", "rep", None),
        P("shard", None, None),
        P("shard", None),
    )
    return jax.shard_map(
        per_device,
        mesh=mesh,
        in_specs=placed,
        out_specs=(P("shard", "rep", None), P("shard", None, None)),
        check_vma=False,
    )
```

```python
import functools

import jax
import jax.numpy as jnp
from jax import lax
from jax.experimental import pallas as pl
from jax.experimental.pallas import tpu as pltpu
from jax.sharding import PartitionSpec as P

learn_rate = 0.5
RELAYS = 4
SKIP = 1
KINDS = "IPTWA"
MESH = pl.DeviceIdType.MESH


def loop(count, body):
    if count <= 8:
        for i in range(count):
            body(i)
    else:

        @pl.loop(0, count)
        def _(i):
            body(i)


def paired(me, i, count):
    if count & (count - 1):
        return lax.rem(me + i, count)
    out, bit = 0, 1
    while bit < count:
        a = (me // bit) % 2
        b = (i // bit) % 2
        out = out + bit * ((a + b) % 2)
        bit *= 2
    return out


def far_of(reps):
    return reps - 1 if reps > 2 else reps


def plan(reps):
    def send(j):
        return ("P", j)

    def ids(j):
        return ("I", j)

    def weigh(g):
        return ("T", g)

    def take(g):
        return ("W", g), ("A", g)

    if reps == 4:
        steps = [
            [weigh(0), send(0), ids(1), ids(2), send(2), ids(3), send(1), ('W',0), ('A',0), weigh(1), ('W',1), ('A',1), weigh(2), ('W',2), ('A',2), weigh(3), ('W',3), ('A',3)],
            [ids(0), send(0), weigh(1), ids(2), ids(3), send(3), send(2), send(1), ('W',3), weigh(0), weigh(2), weigh(3), ('A',3), ('W',1), ('A',1), ('W',0), ('A',0), ('W',2), ('A',2)],
            [ids(0), ids(1), send(0), send(1), weigh(2), ids(3), send(3), send(2), ('W',0), weigh(1), weigh(3), weigh(0), ('A',0), ('W',2), ('A',2), ('W',3), ('A',3), ('W',1), ('A',1)],
            [ids(2), ids(1), ids(0), send(1), send(2), send(0), weigh(3), send(3), weigh(2), weigh(1), weigh(0), ('W',2), ('A',2), ('W',1), ('A',1), ('W',3), ('A',3), ('W',0), ('A',0)],
        ]
    else:
        steps = []
        for z in range(reps):
            low, high = range(z), range(z + 1, reps)
            near = sorted(range(reps), key=lambda g: (abs(g - z), g))
            relayed = [g for g, at in ((reps - 1, 1), (0, reps - 2)) if reps > 2 and z == at]
            row = [ids(j) for j in low] + [send(j) for j in [*reversed(low), z]]
            row += [ids(j) for j in high] + [send(j) for j in high]
            row += [weigh(g) for g in near]
            for g in relayed + [g for g in near if g not in relayed]:
                row += take(g)
            steps.append(row)
    longest = max(len(row) for row in steps)
    rows = []
    for row in steps:
        codes = [KINDS.index(kind) * reps + j for kind, j in row]
        codes += [len(KINDS) * reps] * (longest - len(row))
        base = 1
        while base <= len(KINDS) * reps:
            base *= 2
        held = 1
        while base ** (held + 1) < 2**31:
            held += 1
        words = []
        for at in range(0, longest, held):
            words.append(sum(c * base**n for n, c in enumerate(codes[at : at + held])))
        rows.append(words)
    return longest, base, held, rows


def kernel(
    shards, reps,
    pooled, lengths, slots, weights,
    acc,
    pooled_v, staged, samples, ids_v, tally_v,
    load_sem, send_sem, recv_sem, hop_send, hop_recv, id_send, id_recv, here,
):
    me, z = lax.axis_index("shard"), lax.axis_index("rep")
    per = staged.shape[1]
    height, width = acc.shape
    count = samples.shape[1]
    entries = slots.shape[2]
    far = far_of(reps)
    relays = hop_recv.shape[0]
    group = shards // relays
    rows = group * per
    kept = relays - relays * SKIP // 4 if reps > 2 else relays
    cut = kept * group

    load_pooled = pltpu.make_async_copy(pooled, pooled_v, load_sem.at[0])
    load_ids = []
    for n, (own, at, size) in enumerate(
        ((slots, 0, entries), (weights, entries, entries), (lengths, 2 * entries, count))
    ):
        load_ids.append(
            pltpu.make_async_copy(
                own.at[0], ids_v.at[z, :, pl.ds(at, size)], load_sem.at[1 + n]
            )
        )
    load_pooled.start()
    for copy in load_ids:
        copy.start()

    barrier = pltpu.get_barrier_semaphore()

    def near(j):
        return (j - z < far) & (z - j < far)

    def skips(j):
        return (z == reps - 1) & (j == 0) & (me >= cut)

    def greet(sem, j, i):
        pl.semaphore_signal(
            sem, inc=1, device_id={"shard": paired(me, i, shards), "rep": j}, device_id_type=MESH
        )

    for j in range(reps - 1, 0, -1):

        @pl.when(j > z)
        def _(j=j):
            greet(barrier, j, 0)

            def one(i):
                p = paired(me, i + 1, shards)

                @pl.when(near(j) | ((z == 0) & (p >= cut)))
                def _():
                    greet(barrier, j, i + 1)

            loop(shards - 1, one)

    def greet_mates(sem, above):
        def one(i):
            p = paired(me, i + 1, shards)

            @pl.when((p > me) if above else (p < me))
            def _():
                greet(sem, z, i + 1)

        loop(shards - 1, one)

    greet_mates(barrier, True)
    below = me
    for j in range(reps - 1):
        below = below + jnp.where(j < z, jnp.where(near(j) | skips(j), shards, 1), 0)

    @pl.when(below > 0)
    def _():
        pl.semaphore_wait(barrier, below)

    for j in range(reps - 1):

        @pl.when(j < z)
        def _(j=j):
            greet(here.at[z], j, 0)

            @pl.when(near(j))
            def _():
                loop(shards - 1, lambda i: greet(here.at[z], j, i + 1))

    greet_mates(here.at[z], False)

    load_pooled.wait()

    def stage(t):
        staged[t] = pooled_v[:, 0, t, :]

    loop(shards, stage)
    for copy in load_ids:
        copy.wait()

    def id_copy(g, peer):
        return pltpu.make_async_remote_copy(
            src_ref=ids_v.at[g],
            dst_ref=ids_v.at[g],
            send_sem=id_send.at[peer],
            recv_sem=id_recv.at[g],
            device_id={"rep": peer},
            device_id_type=MESH,
        )

    def piece(g, src, j, dst):
        return pltpu.make_async_remote_copy(
            src_ref=staged.at[dst],
            dst_ref=samples.at[g, pl.ds(pl.multiple_of(src * per, per), per), :],
            send_sem=send_sem.at[j, dst],
            recv_sem=recv_sem.at[g, src],
            device_id={"shard": dst, "rep": j},
            device_id_type=MESH,
        )

    def hop(g, c, peer):
        part = samples.at[g, pl.ds(pl.multiple_of(c * rows, rows), rows), :]
        return pltpu.make_async_remote_copy(
            src_ref=part,
            dst_ref=part,
            send_sem=hop_send.at[peer, c],
            recv_sem=hop_recv.at[c],
            device_id={"rep": peer},
            device_id_type=MESH,
        )

    def each_piece(j, body):
        @pl.when(near(j) | skips(j))
        def _():
            def one(i):
                body(paired(me, shards - 1 - i, shards))

            loop(shards - 1, one)

            @pl.when(j != z)
            def _():
                body(me)

    def send_ids(j):
        @pl.when(j > z)
        def _():
            pl.semaphore_wait(here.at[j], jnp.where(near(j), shards, 1))

        id_copy(z, j).start()

    def send_pieces(j):
        @pl.when((j == z) & (me < shards - 1))
        def _():
            pl.semaphore_wait(here.at[j], shards - 1 - me)

        each_piece(j, lambda p: piece(z, me, j, p).start())

    samples[z, pl.ds(pl.multiple_of(me * per, per), per), :] = staged[me]
    acc[...] = jnp.zeros_like(acc)

    def tally(g):
        @pl.when(g != z)
        def _():
            id_copy(g, g).wait_recv()

        span = min(512, entries)
        lens = ids_v[g, :, pl.ds(2 * entries, count)].astype(jnp.float32)
        ii = lax.broadcasted_iota(jnp.int32, (count, count), 0)
        jj = lax.broadcasted_iota(jnp.int32, (count, count), 1)
        ends = jnp.sum(jnp.where(jj <= ii, lens, 0.0), axis=1, keepdims=True).astype(jnp.int32)
        starts = jnp.sum(jnp.where(jj < ii, lens, 0.0), axis=1, keepdims=True).astype(jnp.int32)
        starts = jnp.broadcast_to(starts, (count, span)).astype(jnp.int16)
        ends = jnp.broadcast_to(ends, (count, span)).astype(jnp.int16)
        ids = lax.broadcasted_iota(jnp.int16, (height, span), 0)

        def rows_of(x, rows, dtype):
            return jnp.concatenate([jnp.broadcast_to(x, (16, span)).astype(dtype)] * (rows // 16), 0)

        def block(b, total):
            at = pl.multiple_of(b * span, span)
            target = rows_of(ids_v[g, :, pl.ds(at, span)], height, jnp.int16)
            factor = ids_v[g, :, pl.ds(entries + at, span)].astype(jnp.float32) * 0.0625
            factor = rows_of(factor, height, jnp.bfloat16)
            pos = rows_of(at + lax.broadcasted_iota(jnp.int32, (1, span), 1), count, jnp.int16)
            one, none = jnp.bfloat16(1), jnp.bfloat16(0)
            member = jnp.where((pos >= starts) & (pos < ends), one, none)
            chosen = jnp.where(ids == target, factor, none)
            return total + lax.dot_general(
                chosen, member, (((1,), (1,)), ((), ())), preferred_element_type=jnp.float32
            )

        total = jnp.zeros((height, count), jnp.float32)
        if entries // span <= 4:
            for b in range(entries // span):
                total = block(b, total)
        else:
            total = lax.fori_loop(0, entries // span, block, total)
        high = total.astype(jnp.bfloat16)
        low = (total - high.astype(jnp.float32)).astype(jnp.bfloat16)
        tally_v[g, :, :count] = high
        tally_v[g, :, count:] = low

    def relay_to(g):
        down = (z == 1) & (g == reps - 1)
        up = (z == reps - 2) & (g == 0)
        return (down | up) if reps > 2 else False, jnp.where(down, 0, reps - 1)

    def arrive(g):
        relay, peer = relay_to(g)

        def part(i):
            c = paired(me // group, relays - 1 - i, relays)

            def one(q):
                src = c * group + q

                @pl.when((g != z) | (src != me))
                def _():
                    piece(g, src, z, src).wait_recv()

            loop(group, one)
            if reps > 2:

                @pl.when(relay & ((c < kept) | (g == 0)))
                def _():
                    hop(g, c, peer).start()

        @pl.when(near(g))
        def _():
            loop(relays, part)

        if reps > 2:

            @pl.when(jnp.logical_not(near(g)))
            def _():
                loop(kept, lambda c: hop(g, c, g).wait_recv())

                @pl.when(z == 0)
                def _():
                    loop(shards - cut, lambda i: piece(g, cut + i, z, cut + i).wait_recv())

                @pl.when(z != 0)
                def _():
                    loop(relays - kept, lambda i: hop(g, kept + i, g).wait_recv())

    def add(g):
        rest = samples[g]
        total = None
        for _ in range(2):
            part = rest.astype(jnp.bfloat16)
            rest = rest - part.astype(jnp.float32)
            term = jnp.dot(
                tally_v[g],
                jnp.concatenate([part, part], axis=0),
                preferred_element_type=jnp.float32,
            )
            total = term if total is None else total + term
        acc[...] += total

    longest, base, held, rows_of_steps = plan(reps)
    words = []
    for n in range(len(rows_of_steps[0])):
        word = rows_of_steps[0][n]
        for row in range(1, reps):
            word = jnp.where(z == row, rows_of_steps[row][n], word)
        words.append(jnp.int32(word))

    def step(k, words):
        code = lax.rem(words[0], base)
        kind, j = lax.div(code, reps), lax.rem(code, reps)
        for at, act in enumerate((send_ids, send_pieces, tally, arrive, add)):

            @pl.when(kind == at)
            def _(act=act):
                act(j)

        over = lax.rem(k, held) == held - 1
        rest = (lax.div(words[0], base),) + tuple(words[1:])
        moved = tuple(words[1:]) + (words[0],)
        return tuple(jnp.where(over, b, a) for a, b in zip(rest, moved))

    lax.fori_loop(0, longest, step, tuple(words))

    for j in range(reps):
        each_piece(j, lambda p: piece(z, me, j, p).wait_send())

        @pl.when(j != z)
        def _(j=j):
            id_copy(z, j).wait_send()

    if reps > 2:
        for g, at, peer in ((reps - 1, 1, 0), (0, reps - 2, reps - 1)):

            @pl.when(z == at)
            def _(g=g, peer=peer):
                loop(kept if g else relays, lambda c: hop(g, c, peer).wait_send())


def finish(reps, acc, touched, state, grad_out, rows_out, rows_v, sems):
    z = lax.axis_index("rep")
    height, width = acc.shape
    part = height // reps
    own = acc.at[pl.ds(pl.multiple_of(z * part, part), part), :]
    copies = [pltpu.make_async_copy(own, grad_out.at[0], sems.at[0])]
    copies[0].start()
    block = min(128, height)
    ii = lax.broadcasted_iota(jnp.int32, (block, block), 0)
    jj = lax.broadcasted_iota(jnp.int32, (block, block), 1)
    for b in range(height // block):
        at = slice(b * block, (b + 1) * block)
        grads = acc[at, :]
        old = jnp.sum(jnp.where(ii == jj, state[:, at], 0.0), axis=1, keepdims=True)
        new = old + jnp.sum(grads * grads, axis=1, keepdims=True) * (1.0 / width)
        rows_v[at, :] = touched[0, at, :] - grads * (learn_rate / (jnp.sqrt(new) + 1e-08))
        to = rows_out.at[0, pl.ds(b * block, block), :]
        copy = pltpu.make_async_copy(rows_v.at[pl.ds(b * block, block), :], to, sems.at[1 + b])
        copy.start()
        copies.append(copy)
    for copy in copies:
        copy.wait()


def per_device(pooled_grad, bag_lengths, row_slots, id_weights, touched_rows, accumulator):
    shards, reps = lax.axis_size("shard"), lax.axis_size("rep")
    per, _, tables, width = pooled_grad.shape
    height = touched_rows.shape[1]
    entries = row_slots.shape[2]
    count = per * shards
    relays = min(RELAYS, shards)
    vmem = pl.BlockSpec(memory_space=pltpu.VMEM)
    hbm = pl.BlockSpec(memory_space=pltpu.HBM)
    dma = pltpu.SemaphoreType.DMA
    sent = [
        pltpu.with_memory_space_constraint(x, pltpu.HBM)
        for x in (pooled_grad, bag_lengths, row_slots, id_weights)
    ]
    total = pl.pallas_call(
        functools.partial(kernel, shards, reps),
        out_shape=jax.ShapeDtypeStruct((height, width), jnp.float32),
        in_specs=[hbm] * 4,
        out_specs=vmem,
        scratch_shapes=[
            pltpu.VMEM((per, 1, tables, width), jnp.float32),
            pltpu.VMEM((tables, per, width), jnp.float32),
            pltpu.VMEM((reps, count, width), jnp.float32),
            pltpu.VMEM((reps, 1, 2 * entries + count), jnp.int32),
            pltpu.VMEM((reps, height, 2 * count), jnp.bfloat16),
            dma((4,)),
            dma((reps, shards)),
            dma((reps, shards)),
            dma((reps, relays)),
            dma((relays,)),
            dma((reps,)),
            dma((reps,)),
            pltpu.SemaphoreType.REGULAR((reps,)),
        ],
        compiler_params=pltpu.CompilerParams(
            collective_id=0, has_side_effects=True, vmem_limit_bytes=40 * 1024 * 1024
        ),
    )(*sent)
    return pl.pallas_call(
        functools.partial(finish, reps),
        out_shape=(
            jax.ShapeDtypeStruct((1, height // reps, width), jnp.float32),
            jax.ShapeDtypeStruct((1, height, width), jnp.float32),
        ),
        in_specs=[vmem] * 3,
        out_specs=(hbm, hbm),
        scratch_shapes=[
            pltpu.VMEM((height, width), jnp.float32),
            dma((1 + height // min(128, height),)),
        ],
        compiler_params=pltpu.CompilerParams(vmem_limit_bytes=16 * 1024 * 1024),
    )(total, touched_rows, accumulator)


def solution(mesh):
    placed = (
        P("shard", "rep", None, None),
        P("shard", "rep", None),
        P("shard", "rep", None),
        P("shard", "rep", None),
        P("shard", None, None),
        P("shard", None),
    )
    return jax.shard_map(
        per_device,
        mesh=mesh,
        in_specs=placed,
        out_specs=(P("shard", "rep", None), P("shard", None, None)),
        check_vma=False,
    )
```

```python
import functools

import jax
import jax.numpy as jnp
from jax import lax
from jax.experimental import pallas as pl
from jax.experimental.pallas import tpu as pltpu
from jax.sharding import PartitionSpec as P

learn_rate = 0.5
RELAYS = 4
SKIP = 3
KINDS = "IPTWA"
MESH = pl.DeviceIdType.MESH


def loop(count, body):
    if count <= 8:
        for i in range(count):
            body(i)
    else:

        @pl.loop(0, count)
        def _(i):
            body(i)


def paired(me, i, count):
    if count & (count - 1):
        return lax.rem(me + i, count)
    out, bit = 0, 1
    while bit < count:
        a = (me // bit) % 2
        b = (i // bit) % 2
        out = out + bit * ((a + b) % 2)
        bit *= 2
    return out


def far_of(reps):
    return reps - 1 if reps > 2 else reps


def plan(reps):
    def send(j):
        return ("P", j)

    def ids(j):
        return ("I", j)

    def weigh(g):
        return ("T", g)

    def take(g):
        return ("W", g), ("A", g)

    if reps == 4:
        steps = [
            [weigh(0), send(0), ids(1), ids(2), send(2), ids(3), send(1), ('W',0), ('A',0), weigh(1), ('W',1), ('A',1), weigh(2), ('W',2), ('A',2), weigh(3), ('W',3), ('A',3)],
            [ids(0), send(0), weigh(1), ids(2), ids(3), send(3), send(2), send(1), ('W',3), weigh(0), weigh(2), weigh(3), ('A',3), ('W',1), ('A',1), ('W',0), ('A',0), ('W',2), ('A',2)],
            [ids(0), ids(1), send(0), send(1), weigh(2), ids(3), send(3), send(2), ('W',0), weigh(1), weigh(3), weigh(0), ('A',0), ('W',2), ('A',2), ('W',3), ('A',3), ('W',1), ('A',1)],
            [ids(2), ids(1), ids(0), send(1), send(2), send(0), weigh(3), send(3), weigh(2), weigh(1), weigh(0), ('W',2), ('A',2), ('W',1), ('A',1), ('W',3), ('A',3), ('W',0), ('A',0)],
        ]
    else:
        steps = []
        for z in range(reps):
            low, high = range(z), range(z + 1, reps)
            near = sorted(range(reps), key=lambda g: (abs(g - z), g))
            relayed = [g for g, at in ((reps - 1, 1), (0, reps - 2)) if reps > 2 and z == at]
            row = [ids(j) for j in low] + [send(j) for j in [*reversed(low), z]]
            row += [ids(j) for j in high] + [send(j) for j in high]
            row += [weigh(g) for g in near]
            for g in relayed + [g for g in near if g not in relayed]:
                row += take(g)
            steps.append(row)
    longest = max(len(row) for row in steps)
    rows = []
    for row in steps:
        codes = [KINDS.index(kind) * reps + j for kind, j in row]
        codes += [len(KINDS) * reps] * (longest - len(row))
        base = 1
        while base <= len(KINDS) * reps:
            base *= 2
        held = 1
        while base ** (held + 1) < 2**31:
            held += 1
        words = []
        for at in range(0, longest, held):
            words.append(sum(c * base**n for n, c in enumerate(codes[at : at + held])))
        rows.append(words)
    return longest, base, held, rows


def kernel(
    shards, reps,
    pooled, lengths, slots, weights,
    acc,
    pooled_v, staged, samples, ids_v, tally_v,
    load_sem, send_sem, recv_sem, hop_send, hop_recv, id_send, id_recv, here,
):
    me, z = lax.axis_index("shard"), lax.axis_index("rep")
    per = staged.shape[1]
    height, width = acc.shape
    count = samples.shape[1]
    entries = slots.shape[2]
    far = far_of(reps)
    relays = hop_recv.shape[0]
    group = shards // relays
    rows = group * per
    kept = relays - relays * SKIP // 4 if reps > 2 else relays
    cut = kept * group

    load_pooled = pltpu.make_async_copy(pooled, pooled_v, load_sem.at[0])
    load_ids = []
    for n, (own, at, size) in enumerate(
        ((slots, 0, entries), (weights, entries, entries), (lengths, 2 * entries, count))
    ):
        load_ids.append(
            pltpu.make_async_copy(
                own.at[0], ids_v.at[z, :, pl.ds(at, size)], load_sem.at[1 + n]
            )
        )
    load_pooled.start()
    for copy in load_ids:
        copy.start()

    barrier = pltpu.get_barrier_semaphore()

    def near(j):
        return (j - z < far) & (z - j < far)

    def skips(j):
        return (z == reps - 1) & (j == 0) & (me >= cut)

    def greet(sem, j, i):
        pl.semaphore_signal(
            sem, inc=1, device_id={"shard": paired(me, i, shards), "rep": j}, device_id_type=MESH
        )

    for j in range(reps - 1, 0, -1):

        @pl.when(j > z)
        def _(j=j):
            greet(barrier, j, 0)

            def one(i):
                p = paired(me, i + 1, shards)

                @pl.when(near(j) | ((z == 0) & (p >= cut) & (me < group)))
                def _():
                    greet(barrier, j, i + 1)

            loop(shards - 1, one)

    def greet_mates(sem, above):
        def one(i):
            p = paired(me, i + 1, shards)

            @pl.when((p > me) if above else (p < me))
            def _():
                greet(sem, z, i + 1)

        loop(shards - 1, one)

    greet_mates(barrier, True)
    below = me
    for j in range(reps - 1):
        below = below + jnp.where(
            j < z, jnp.where(near(j), shards, jnp.where(skips(j), group + 1, 1)), 0
        )

    @pl.when(below > 0)
    def _():
        pl.semaphore_wait(barrier, below)

    for j in range(reps - 1):

        @pl.when(j < z)
        def _(j=j):
            greet(here.at[z], j, 0)

            @pl.when(near(j))
            def _():
                loop(shards - 1, lambda i: greet(here.at[z], j, i + 1))

    greet_mates(here.at[z], False)

    load_pooled.wait()

    def stage(t):
        staged[t] = pooled_v[:, 0, t, :]

    loop(shards, stage)
    for copy in load_ids:
        copy.wait()

    def id_copy(g, peer):
        return pltpu.make_async_remote_copy(
            src_ref=ids_v.at[g],
            dst_ref=ids_v.at[g],
            send_sem=id_send.at[peer],
            recv_sem=id_recv.at[g],
            device_id={"rep": peer},
            device_id_type=MESH,
        )

    def piece(g, src, j, dst):
        return pltpu.make_async_remote_copy(
            src_ref=staged.at[dst],
            dst_ref=samples.at[g, pl.ds(pl.multiple_of(src * per, per), per), :],
            send_sem=send_sem.at[j, dst],
            recv_sem=recv_sem.at[g, src],
            device_id={"shard": dst, "rep": j},
            device_id_type=MESH,
        )

    def hop(g, c, peer):
        part = samples.at[g, pl.ds(pl.multiple_of(c * rows, rows), rows), :]
        return pltpu.make_async_remote_copy(
            src_ref=part,
            dst_ref=part,
            send_sem=hop_send.at[peer, c],
            recv_sem=hop_recv.at[c],
            device_id={"rep": peer},
            device_id_type=MESH,
        )

    def each_piece(j, body):
        @pl.when(near(j) | skips(j))
        def _():
            def one(i):
                p = paired(me, shards - 1 - i, shards)

                @pl.when(near(j) | (p < group))
                def _():
                    body(p)

            loop(shards - 1, one)

            @pl.when((j != z) & near(j))
            def _():
                body(me)

    def send_ids(j):
        @pl.when(j > z)
        def _():
            pl.semaphore_wait(here.at[j], jnp.where(near(j), shards, 1))

        id_copy(z, j).start()

    def send_pieces(j):
        @pl.when((j == z) & (me < shards - 1))
        def _():
            pl.semaphore_wait(here.at[j], shards - 1 - me)

        each_piece(j, lambda p: piece(z, me, j, p).start())

    samples[z, pl.ds(pl.multiple_of(me * per, per), per), :] = staged[me]
    acc[...] = jnp.zeros_like(acc)

    def tally(g):
        @pl.when(g != z)
        def _():
            id_copy(g, g).wait_recv()

        span = min(512, entries)
        lens = ids_v[g, :, pl.ds(2 * entries, count)].astype(jnp.float32)
        ii = lax.broadcasted_iota(jnp.int32, (count, count), 0)
        jj = lax.broadcasted_iota(jnp.int32, (count, count), 1)
        ends = jnp.sum(jnp.where(jj <= ii, lens, 0.0), axis=1, keepdims=True).astype(jnp.int32)
        starts = jnp.sum(jnp.where(jj < ii, lens, 0.0), axis=1, keepdims=True).astype(jnp.int32)
        starts = jnp.broadcast_to(starts, (count, span)).astype(jnp.int16)
        ends = jnp.broadcast_to(ends, (count, span)).astype(jnp.int16)
        ids = lax.broadcasted_iota(jnp.int16, (height, span), 0)

        def rows_of(x, rows, dtype):
            return jnp.concatenate([jnp.broadcast_to(x, (16, span)).astype(dtype)] * (rows // 16), 0)

        def block(b, total):
            at = pl.multiple_of(b * span, span)
            target = rows_of(ids_v[g, :, pl.ds(at, span)], height, jnp.int16)
            factor = ids_v[g, :, pl.ds(entries + at, span)].astype(jnp.float32) * 0.0625
            factor = rows_of(factor, height, jnp.bfloat16)
            pos = rows_of(at + lax.broadcasted_iota(jnp.int32, (1, span), 1), count, jnp.int16)
            one, none = jnp.bfloat16(1), jnp.bfloat16(0)
            member = jnp.where((pos >= starts) & (pos < ends), one, none)
            chosen = jnp.where(ids == target, factor, none)
            return total + lax.dot_general(
                chosen, member, (((1,), (1,)), ((), ())), preferred_element_type=jnp.float32
            )

        total = jnp.zeros((height, count), jnp.float32)
        if entries // span <= 4:
            for b in range(entries // span):
                total = block(b, total)
        else:
            total = lax.fori_loop(0, entries // span, block, total)
        high = total.astype(jnp.bfloat16)
        low = (total - high.astype(jnp.float32)).astype(jnp.bfloat16)
        tally_v[g, :, :count] = high
        tally_v[g, :, count:] = low

    def relayed(g, c):
        return (c < kept) | (g == 0) | (me >= group)

    def relay_to(g):
        down = (z == 1) & (g == reps - 1)
        up = (z == reps - 2) & (g == 0)
        return (down | up) if reps > 2 else False, jnp.where(down, 0, reps - 1)

    def arrive(g):
        relay, peer = relay_to(g)

        def part(i):
            c = paired(me // group, relays - 1 - i, relays)

            def one(q):
                src = c * group + q

                @pl.when((g != z) | (src != me))
                def _():
                    piece(g, src, z, src).wait_recv()

            loop(group, one)
            if reps > 2:

                @pl.when(relay & relayed(g, c))
                def _():
                    hop(g, c, peer).start()

        @pl.when(near(g))
        def _():
            loop(relays, part)

        if reps > 2:

            @pl.when(jnp.logical_not(near(g)))
            def _():
                def whole(c):
                    @pl.when(relayed(g, c))
                    def _():
                        hop(g, c, g).wait_recv()

                loop(relays, whole)

                @pl.when((z == 0) & (me < group))
                def _():
                    loop(shards - cut, lambda i: piece(g, cut + i, z, cut + i).wait_recv())

    def add(g):
        rest = samples[g]
        total = None
        for _ in range(2):
            part = rest.astype(jnp.bfloat16)
            rest = rest - part.astype(jnp.float32)
            term = jnp.dot(
                tally_v[g],
                jnp.concatenate([part, part], axis=0),
                preferred_element_type=jnp.float32,
            )
            total = term if total is None else total + term
        acc[...] += total

    longest, base, held, rows_of_steps = plan(reps)
    words = []
    for n in range(len(rows_of_steps[0])):
        word = rows_of_steps[0][n]
        for row in range(1, reps):
            word = jnp.where(z == row, rows_of_steps[row][n], word)
        words.append(jnp.int32(word))

    def step(k, words):
        code = lax.rem(words[0], base)
        kind, j = lax.div(code, reps), lax.rem(code, reps)
        for at, act in enumerate((send_ids, send_pieces, tally, arrive, add)):

            @pl.when(kind == at)
            def _(act=act):
                act(j)

        over = lax.rem(k, held) == held - 1
        rest = (lax.div(words[0], base),) + tuple(words[1:])
        moved = tuple(words[1:]) + (words[0],)
        return tuple(jnp.where(over, b, a) for a, b in zip(rest, moved))

    lax.fori_loop(0, longest, step, tuple(words))

    for j in range(reps):
        each_piece(j, lambda p: piece(z, me, j, p).wait_send())

        @pl.when(j != z)
        def _(j=j):
            id_copy(z, j).wait_send()

    if reps > 2:
        for g, at, peer in ((reps - 1, 1, 0), (0, reps - 2, reps - 1)):

            @pl.when(z == at)
            def _(g=g, peer=peer):
                def left(c):
                    @pl.when(relayed(g, c))
                    def _():
                        hop(g, c, peer).wait_send()

                loop(relays, left)


def finish(reps, acc, touched, state, grad_out, rows_out, rows_v, sems):
    z = lax.axis_index("rep")
    height, width = acc.shape
    part = height // reps
    own = acc.at[pl.ds(pl.multiple_of(z * part, part), part), :]
    copies = [pltpu.make_async_copy(own, grad_out.at[0], sems.at[0])]
    copies[0].start()
    block = min(128, height)
    ii = lax.broadcasted_iota(jnp.int32, (block, block), 0)
    jj = lax.broadcasted_iota(jnp.int32, (block, block), 1)
    for b in range(height // block):
        at = slice(b * block, (b + 1) * block)
        grads = acc[at, :]
        old = jnp.sum(jnp.where(ii == jj, state[:, at], 0.0), axis=1, keepdims=True)
        new = old + jnp.sum(grads * grads, axis=1, keepdims=True) * (1.0 / width)
        rows_v[at, :] = touched[0, at, :] - grads * (learn_rate / (jnp.sqrt(new) + 1e-08))
        to = rows_out.at[0, pl.ds(b * block, block), :]
        copy = pltpu.make_async_copy(rows_v.at[pl.ds(b * block, block), :], to, sems.at[1 + b])
        copy.start()
        copies.append(copy)
    for copy in copies:
        copy.wait()


def per_device(pooled_grad, bag_lengths, row_slots, id_weights, touched_rows, accumulator):
    shards, reps = lax.axis_size("shard"), lax.axis_size("rep")
    per, _, tables, width = pooled_grad.shape
    height = touched_rows.shape[1]
    entries = row_slots.shape[2]
    count = per * shards
    relays = min(RELAYS, shards)
    vmem = pl.BlockSpec(memory_space=pltpu.VMEM)
    hbm = pl.BlockSpec(memory_space=pltpu.HBM)
    dma = pltpu.SemaphoreType.DMA
    sent = [
        pltpu.with_memory_space_constraint(x, pltpu.HBM)
        for x in (pooled_grad, bag_lengths, row_slots, id_weights)
    ]
    total = pl.pallas_call(
        functools.partial(kernel, shards, reps),
        out_shape=jax.ShapeDtypeStruct((height, width), jnp.float32),
        in_specs=[hbm] * 4,
        out_specs=vmem,
        scratch_shapes=[
            pltpu.VMEM((per, 1, tables, width), jnp.float32),
            pltpu.VMEM((tables, per, width), jnp.float32),
            pltpu.VMEM((reps, count, width), jnp.float32),
            pltpu.VMEM((reps, 1, 2 * entries + count), jnp.int32),
            pltpu.VMEM((reps, height, 2 * count), jnp.bfloat16),
            dma((4,)),
            dma((reps, shards)),
            dma((reps, shards)),
            dma((reps, relays)),
            dma((relays,)),
            dma((reps,)),
            dma((reps,)),
            pltpu.SemaphoreType.REGULAR((reps,)),
        ],
        compiler_params=pltpu.CompilerParams(
            collective_id=0, has_side_effects=True, vmem_limit_bytes=40 * 1024 * 1024
        ),
    )(*sent)
    return pl.pallas_call(
        functools.partial(finish, reps),
        out_shape=(
            jax.ShapeDtypeStruct((1, height // reps, width), jnp.float32),
            jax.ShapeDtypeStruct((1, height, width), jnp.float32),
        ),
        in_specs=[vmem] * 3,
        out_specs=(hbm, hbm),
        scratch_shapes=[
            pltpu.VMEM((height, width), jnp.float32),
            dma((1 + height // min(128, height),)),
        ],
        compiler_params=pltpu.CompilerParams(vmem_limit_bytes=16 * 1024 * 1024),
    )(total, touched_rows, accumulator)


def solution(mesh):
    placed = (
        P("shard", "rep", None, None),
        P("shard", "rep", None),
        P("shard", "rep", None),
        P("shard", "rep", None),
        P("shard", None, None),
        P("shard", None),
    )
    return jax.shard_map(
        per_device,
        mesh=mesh,
        in_specs=placed,
        out_specs=(P("shard", "rep", None), P("shard", None, None)),
        check_vma=False,
    )
```

```python
import functools

import jax
import jax.numpy as jnp
from jax import lax
from jax.experimental import pallas as pl
from jax.experimental.pallas import tpu as pltpu
from jax.sharding import PartitionSpec as P

learn_rate = 0.5
RELAYS = 4
SKIP = 3
KINDS = "IPTWA"
MESH = pl.DeviceIdType.MESH


def loop(count, body):
    if count <= 8:
        for i in range(count):
            body(i)
    else:

        @pl.loop(0, count)
        def _(i):
            body(i)


def paired(me, i, count):
    if count & (count - 1):
        return lax.rem(me + i, count)
    out, bit = 0, 1
    while bit < count:
        a = (me // bit) % 2
        b = (i // bit) % 2
        out = out + bit * ((a + b) % 2)
        bit *= 2
    return out


def far_of(reps):
    return reps - 1 if reps > 2 else reps


def plan(reps):
    def send(j):
        return ("P", j)

    def ids(j):
        return ("I", j)

    def weigh(g):
        return ("T", g)

    def take(g):
        return ("W", g), ("A", g)

    if reps == 4:
        steps = [
            [weigh(0), send(0), ids(1), ids(2), send(2), ids(3), send(1), ('W',0), ('A',0), weigh(1), ('W',1), ('A',1), weigh(2), weigh(3), ('W',2), ('A',2), ('W',3), ('A',3)],
            [ids(0), send(0), weigh(1), ids(2), ids(3), send(3), send(2), send(1), ('W',3), weigh(0), weigh(2), weigh(3), ('A',3), ('W',1), ('A',1), ('W',0), ('A',0), ('W',2), ('A',2)],
            [ids(0), ids(1), send(0), send(1), weigh(2), ids(3), send(3), send(2), ('W',0), weigh(1), weigh(3), weigh(0), ('A',0), ('W',2), ('A',2), ('W',3), ('A',3), ('W',1), ('A',1)],
            [ids(2), ids(1), ids(0), send(1), send(2), send(0), weigh(3), send(3), weigh(2), weigh(1), weigh(0), ('W',2), ('A',2), ('W',1), ('A',1), ('W',3), ('A',3), ('W',0), ('A',0)],
        ]
    else:
        steps = []
        for z in range(reps):
            low, high = range(z), range(z + 1, reps)
            near = sorted(range(reps), key=lambda g: (abs(g - z), g))
            relayed = [g for g, at in ((reps - 1, 1), (0, reps - 2)) if reps > 2 and z == at]
            row = [ids(j) for j in low] + [send(j) for j in [*reversed(low), z]]
            row += [ids(j) for j in high] + [send(j) for j in high]
            row += [weigh(g) for g in near]
            for g in relayed + [g for g in near if g not in relayed]:
                row += take(g)
            steps.append(row)
    longest = max(len(row) for row in steps)
    rows = []
    for row in steps:
        codes = [KINDS.index(kind) * reps + j for kind, j in row]
        codes += [len(KINDS) * reps] * (longest - len(row))
        base = 1
        while base <= len(KINDS) * reps:
            base *= 2
        held = 1
        while base ** (held + 1) < 2**31:
            held += 1
        words = []
        for at in range(0, longest, held):
            words.append(sum(c * base**n for n, c in enumerate(codes[at : at + held])))
        rows.append(words)
    return longest, base, held, rows


def kernel(
    shards, reps,
    pooled, lengths, slots, weights,
    acc,
    pooled_v, staged, samples, ids_v, tally_v,
    load_sem, send_sem, recv_sem, hop_send, hop_recv, id_send, id_recv, here,
):
    me, z = lax.axis_index("shard"), lax.axis_index("rep")
    per = staged.shape[1]
    height, width = acc.shape
    count = samples.shape[1]
    entries = slots.shape[2]
    far = far_of(reps)
    relays = hop_recv.shape[0]
    group = shards // relays
    rows = group * per
    kept = relays - relays * SKIP // 4 if reps > 2 else relays
    cut = kept * group

    load_pooled = pltpu.make_async_copy(pooled, pooled_v, load_sem.at[0])
    load_ids = []
    for n, (own, at, size) in enumerate(
        ((slots, 0, entries), (weights, entries, entries), (lengths, 2 * entries, count))
    ):
        load_ids.append(
            pltpu.make_async_copy(
                own.at[0], ids_v.at[z, :, pl.ds(at, size)], load_sem.at[1 + n]
            )
        )
    load_pooled.start()
    for copy in load_ids:
        copy.start()

    barrier = pltpu.get_barrier_semaphore()

    def near(j):
        return (j - z < far) & (z - j < far)

    def skips(j):
        return (z == reps - 1) & (j == 0) & (me >= cut)

    def greet(sem, j, i):
        pl.semaphore_signal(
            sem, inc=1, device_id={"shard": paired(me, i, shards), "rep": j}, device_id_type=MESH
        )

    for j in range(reps - 1, 0, -1):

        @pl.when(j > z)
        def _(j=j):
            greet(barrier, j, 0)

            def one(i):
                p = paired(me, i + 1, shards)

                @pl.when(near(j) | ((z == 0) & (p >= cut) & (me < group)))
                def _():
                    greet(barrier, j, i + 1)

            loop(shards - 1, one)

    def greet_mates(sem, above):
        def one(i):
            p = paired(me, i + 1, shards)

            @pl.when((p > me) if above else (p < me))
            def _():
                greet(sem, z, i + 1)

        loop(shards - 1, one)

    greet_mates(barrier, True)
    below = me
    for j in range(reps - 1):
        below = below + jnp.where(
            j < z, jnp.where(near(j), shards, jnp.where(skips(j), group + 1, 1)), 0
        )

    @pl.when(below > 0)
    def _():
        pl.semaphore_wait(barrier, below)

    for j in range(reps - 1):

        @pl.when(j < z)
        def _(j=j):
            greet(here.at[z], j, 0)

            @pl.when(near(j))
            def _():
                loop(shards - 1, lambda i: greet(here.at[z], j, i + 1))

    greet_mates(here.at[z], False)

    load_pooled.wait()

    def stage(t):
        staged[t] = pooled_v[:, 0, t, :]

    loop(shards, stage)
    for copy in load_ids:
        copy.wait()

    def id_copy(g, peer):
        return pltpu.make_async_remote_copy(
            src_ref=ids_v.at[g],
            dst_ref=ids_v.at[g],
            send_sem=id_send.at[peer],
            recv_sem=id_recv.at[g],
            device_id={"rep": peer},
            device_id_type=MESH,
        )

    def piece(g, src, j, dst):
        return pltpu.make_async_remote_copy(
            src_ref=staged.at[dst],
            dst_ref=samples.at[g, pl.ds(pl.multiple_of(src * per, per), per), :],
            send_sem=send_sem.at[j, dst],
            recv_sem=recv_sem.at[g, src],
            device_id={"shard": dst, "rep": j},
            device_id_type=MESH,
        )

    def hop(g, c, peer):
        part = samples.at[g, pl.ds(pl.multiple_of(c * rows, rows), rows), :]
        return pltpu.make_async_remote_copy(
            src_ref=part,
            dst_ref=part,
            send_sem=hop_send.at[peer, c],
            recv_sem=hop_recv.at[c],
            device_id={"rep": peer},
            device_id_type=MESH,
        )

    def each_piece(j, body):
        @pl.when(near(j) | skips(j))
        def _():
            def one(i):
                p = paired(me, shards - 1 - i, shards)

                @pl.when(near(j) | (p < group))
                def _():
                    body(p)

            loop(shards - 1, one)

            @pl.when((j != z) & near(j))
            def _():
                body(me)

    def send_ids(j):
        @pl.when(j > z)
        def _():
            pl.semaphore_wait(here.at[j], jnp.where(near(j), shards, 1))

        id_copy(z, j).start()

    def send_pieces(j):
        @pl.when((j == z) & (me < shards - 1))
        def _():
            pl.semaphore_wait(here.at[j], shards - 1 - me)

        each_piece(j, lambda p: piece(z, me, j, p).start())

    samples[z, pl.ds(pl.multiple_of(me * per, per), per), :] = staged[me]
    acc[...] = jnp.zeros_like(acc)

    def tally(g):
        @pl.when(g != z)
        def _():
            id_copy(g, g).wait_recv()

        span = min(512, entries)
        lens = ids_v[g, :, pl.ds(2 * entries, count)].astype(jnp.float32)
        ii = lax.broadcasted_iota(jnp.int32, (count, count), 0)
        jj = lax.broadcasted_iota(jnp.int32, (count, count), 1)
        ends = jnp.sum(jnp.where(jj <= ii, lens, 0.0), axis=1, keepdims=True).astype(jnp.int32)
        starts = jnp.sum(jnp.where(jj < ii, lens, 0.0), axis=1, keepdims=True).astype(jnp.int32)
        starts = jnp.broadcast_to(starts, (count, span)).astype(jnp.int16)
        ends = jnp.broadcast_to(ends, (count, span)).astype(jnp.int16)
        ids = lax.broadcasted_iota(jnp.int16, (height, span), 0)

        def rows_of(x, rows, dtype):
            return jnp.concatenate([jnp.broadcast_to(x, (16, span)).astype(dtype)] * (rows // 16), 0)

        def block(b, total):
            at = pl.multiple_of(b * span, span)
            target = rows_of(ids_v[g, :, pl.ds(at, span)], height, jnp.int16)
            factor = ids_v[g, :, pl.ds(entries + at, span)].astype(jnp.float32) * 0.0625
            factor = rows_of(factor, height, jnp.bfloat16)
            pos = rows_of(at + lax.broadcasted_iota(jnp.int32, (1, span), 1), count, jnp.int16)
            one, none = jnp.bfloat16(1), jnp.bfloat16(0)
            member = jnp.where((pos >= starts) & (pos < ends), one, none)
            chosen = jnp.where(ids == target, factor, none)
            return total + lax.dot_general(
                chosen, member, (((1,), (1,)), ((), ())), preferred_element_type=jnp.float32
            )

        total = jnp.zeros((height, count), jnp.float32)
        if entries // span <= 4:
            for b in range(entries // span):
                total = block(b, total)
        else:
            total = lax.fori_loop(0, entries // span, block, total)
        high = total.astype(jnp.bfloat16)
        low = (total - high.astype(jnp.float32)).astype(jnp.bfloat16)
        tally_v[g, :, :count] = high
        tally_v[g, :, count:] = low

    def relayed(g, c):
        return (c < kept) | (g == 0) | (me >= group)

    def relay_to(g):
        down = (z == 1) & (g == reps - 1)
        up = (z == reps - 2) & (g == 0)
        return (down | up) if reps > 2 else False, jnp.where(down, 0, reps - 1)

    def arrive(g):
        relay, peer = relay_to(g)

        def part(i):
            c = paired(me // group, relays - 1 - i, relays)

            def one(q):
                src = c * group + q

                @pl.when((g != z) | (src != me))
                def _():
                    piece(g, src, z, src).wait_recv()

            loop(group, one)
            if reps > 2:

                @pl.when(relay & relayed(g, c))
                def _():
                    hop(g, c, peer).start()

        @pl.when(near(g))
        def _():
            loop(relays, part)

        if reps > 2:

            @pl.when(jnp.logical_not(near(g)))
            def _():
                def whole(c):
                    @pl.when(relayed(g, c))
                    def _():
                        hop(g, c, g).wait_recv()

                loop(relays, whole)

                @pl.when((z == 0) & (me < group))
                def _():
                    loop(shards - cut, lambda i: piece(g, cut + i, z, cut + i).wait_recv())

    def add(g):
        rest = samples[g]
        total = None
        for _ in range(2):
            part = rest.astype(jnp.bfloat16)
            rest = rest - part.astype(jnp.float32)
            term = jnp.dot(
                tally_v[g],
                jnp.concatenate([part, part], axis=0),
                preferred_element_type=jnp.float32,
            )
            total = term if total is None else total + term
        acc[...] += total

    longest, base, held, rows_of_steps = plan(reps)
    words = []
    for n in range(len(rows_of_steps[0])):
        word = rows_of_steps[0][n]
        for row in range(1, reps):
            word = jnp.where(z == row, rows_of_steps[row][n], word)
        words.append(jnp.int32(word))

    def step(k, words):
        code = lax.rem(words[0], base)
        kind, j = lax.div(code, reps), lax.rem(code, reps)
        for at, act in enumerate((send_ids, send_pieces, tally, arrive, add)):

            @pl.when(kind == at)
            def _(act=act):
                act(j)

        over = lax.rem(k, held) == held - 1
        rest = (lax.div(words[0], base),) + tuple(words[1:])
        moved = tuple(words[1:]) + (words[0],)
        return tuple(jnp.where(over, b, a) for a, b in zip(rest, moved))

    lax.fori_loop(0, longest, step, tuple(words))

    for j in range(reps):
        each_piece(j, lambda p: piece(z, me, j, p).wait_send())

        @pl.when(j != z)
        def _(j=j):
            id_copy(z, j).wait_send()

    if reps > 2:
        for g, at, peer in ((reps - 1, 1, 0), (0, reps - 2, reps - 1)):

            @pl.when(z == at)
            def _(g=g, peer=peer):
                def left(c):
                    @pl.when(relayed(g, c))
                    def _():
                        hop(g, c, peer).wait_send()

                loop(relays, left)


def finish(reps, acc, touched, state, grad_out, rows_out, rows_v, sems):
    z = lax.axis_index("rep")
    height, width = acc.shape
    part = height // reps
    own = acc.at[pl.ds(pl.multiple_of(z * part, part), part), :]
    copies = [pltpu.make_async_copy(own, grad_out.at[0], sems.at[0])]
    copies[0].start()
    block = min(128, height)
    ii = lax.broadcasted_iota(jnp.int32, (block, block), 0)
    jj = lax.broadcasted_iota(jnp.int32, (block, block), 1)
    for b in range(height // block):
        at = slice(b * block, (b + 1) * block)
        grads = acc[at, :]
        old = jnp.sum(jnp.where(ii == jj, state[:, at], 0.0), axis=1, keepdims=True)
        new = old + jnp.sum(grads * grads, axis=1, keepdims=True) * (1.0 / width)
        rows_v[at, :] = touched[0, at, :] - grads * (learn_rate / (jnp.sqrt(new) + 1e-08))
        to = rows_out.at[0, pl.ds(b * block, block), :]
        copy = pltpu.make_async_copy(rows_v.at[pl.ds(b * block, block), :], to, sems.at[1 + b])
        copy.start()
        copies.append(copy)
    for copy in copies:
        copy.wait()


def per_device(pooled_grad, bag_lengths, row_slots, id_weights, touched_rows, accumulator):
    shards, reps = lax.axis_size("shard"), lax.axis_size("rep")
    per, _, tables, width = pooled_grad.shape
    height = touched_rows.shape[1]
    entries = row_slots.shape[2]
    count = per * shards
    relays = min(RELAYS, shards)
    vmem = pl.BlockSpec(memory_space=pltpu.VMEM)
    hbm = pl.BlockSpec(memory_space=pltpu.HBM)
    dma = pltpu.SemaphoreType.DMA
    sent = [
        pltpu.with_memory_space_constraint(x, pltpu.HBM)
        for x in (pooled_grad, bag_lengths, row_slots, id_weights)
    ]
    total = pl.pallas_call(
        functools.partial(kernel, shards, reps),
        out_shape=jax.ShapeDtypeStruct((height, width), jnp.float32),
        in_specs=[hbm] * 4,
        out_specs=vmem,
        scratch_shapes=[
            pltpu.VMEM((per, 1, tables, width), jnp.float32),
            pltpu.VMEM((tables, per, width), jnp.float32),
            pltpu.VMEM((reps, count, width), jnp.float32),
            pltpu.VMEM((reps, 1, 2 * entries + count), jnp.int32),
            pltpu.VMEM((reps, height, 2 * count), jnp.bfloat16),
            dma((4,)),
            dma((reps, shards)),
            dma((reps, shards)),
            dma((reps, relays)),
            dma((relays,)),
            dma((reps,)),
            dma((reps,)),
            pltpu.SemaphoreType.REGULAR((reps,)),
        ],
        compiler_params=pltpu.CompilerParams(
            collective_id=0, has_side_effects=True, vmem_limit_bytes=40 * 1024 * 1024
        ),
    )(*sent)
    return pl.pallas_call(
        functools.partial(finish, reps),
        out_shape=(
            jax.ShapeDtypeStruct((1, height // reps, width), jnp.float32),
            jax.ShapeDtypeStruct((1, height, width), jnp.float32),
        ),
        in_specs=[vmem] * 3,
        out_specs=(hbm, hbm),
        scratch_shapes=[
            pltpu.VMEM((height, width), jnp.float32),
            dma((1 + height // min(128, height),)),
        ],
        compiler_params=pltpu.CompilerParams(vmem_limit_bytes=16 * 1024 * 1024),
    )(total, touched_rows, accumulator)


def solution(mesh):
    placed = (
        P("shard", "rep", None, None),
        P("shard", "rep", None),
        P("shard", "rep", None),
        P("shard", "rep", None),
        P("shard", None, None),
        P("shard", None),
    )
    return jax.shard_map(
        per_device,
        mesh=mesh,
        in_specs=placed,
        out_specs=(P("shard", "rep", None), P("shard", None, None)),
        check_vma=False,
    )
```
